256 devices in a mesh: tm: 4 (over z_lo, core), mesh: 64 (over z_hi, x, y).
Axes of the slice: x: 4, y: 4, z: 8 (z_hi: 4, z_lo: 2; z = z_hi * 2 + z_lo), core: 2. Of those that a mesh axis runs over, the one named last changes fastest.
Arguments:
- states: bfloat16 [32, 8192, 256], P('tm', 'mesh'), may hold values from -6 to 6
- increment: float32 [32, 8192, 256], P('tm', 'mesh'), may hold values from -6 to 6
- window_slots: int32 [64, 4], P('mesh'), may hold values from 0 to 2, as said below
- edge_weights: bfloat16 [2, 64, 4, 128, 128], P(None, 'mesh'), may hold values from -0.125 to 0.125
- inner_weight: bfloat16 [2, 256, 1024], replicated, may hold values from -0.375 to 0.375
- inner_bias: float32 [2, 1024], replicated, may hold values from -5 to 5
- outer_weight: bfloat16 [2, 1024, 256], replicated, may hold values from -0.1875 to 0.1875
Outputs:
- misfit: float32 [32, 8192, 256], P('tm', 'mesh')
- normal_product: float32 [32, 8192, 256], P('tm', 'mesh')
The draws below stay inside these ranges and needn't reach their ends.
Inputs may be any that keep to these rules, and one draw needn't show every extreme that they name: `window_slots`: slot 0 of a block's window is the block of the previous partition along mesh (cyclically), slot 1 the partition's own block, slot 2 the block of the next partition; every block's list names slot 0 and slot 2 at least once, and may name a slot twice.
All inputs are finite; a program needn't handle non-finite values.
Results may differ from the reference program's by a relative error of at most 0.007.
Values may be sent and summed in bfloat16 or wider, within the bound.
No kernel may reach another device: no remote copies, remote signals or barrier semaphores. Data moves between devices by JAX's collectives and lax.ppermute only.
A program may use at most 64 MiB of HBM per device.

```python
import jax
import jax.numpy as jnp
from jax import lax

D = 256
HID = 1024
BLOCK = 128
FANOUT = 4
LAYERS = 2
BLK_DEV = 1
BLOCKS = 64
NODES = 8192
SUBWIN = 32


def draw_window_slots(key, part):
    key_values, key_rotate = jax.random.split(key)
    entries = jax.random.randint(key_values, (BLOCKS, FANOUT), 0, BLK_DEV + 2, dtype=jnp.int32)
    columns = jnp.arange(FANOUT, dtype=jnp.int32)[None, :]
    entries = jnp.where(columns == 0, jnp.int32(0), jnp.where(columns == 1, jnp.int32(BLK_DEV + 1), entries))
    rotation = jax.random.randint(key_rotate, (BLOCKS, 1), 0, FANOUT, dtype=jnp.int32)
    ordering = jnp.mod(columns + rotation, FANOUT).astype(jnp.int32)
    return jnp.take_along_axis(entries, ordering, axis=1)


def shard_levels(stream_key, shape, cuts, low, high):
    level = 1.0
    for position, shards_of in cuts:
        steps = jax.random.uniform(jax.random.fold_in(jax.random.fold_in(stream_key, 6), position), (shards_of,), jnp.float32, low / len(cuts), high / len(cuts))
        level = level * jnp.repeat(jnp.exp(steps), shape[position] // shards_of).reshape((-1,) + (1,) * (len(shape) - 1 - position))
    return level


def scatter_about(stream_key, dims, width, reach, cuts=(), held_as=jnp.bfloat16):
    gain = shard_levels(stream_key, dims, cuts, -0.22, 0.18) if cuts else 1.0
    drawn = jax.random.normal(stream_key, dims, jnp.float32) * width * gain
    return jnp.minimum(jnp.maximum(drawn, -reach), reach).astype(held_as)


def setup_inputs(seed: int = 0) -> dict:
    key_list = jax.random.split(jax.random.key(seed), 8)
    return {
        "states": scatter_about(key_list[0], (SUBWIN, NODES, D), 1.0, 6.0, ((0, 4), (1, 64))),
        "increment": scatter_about(key_list[1], (SUBWIN, NODES, D), 1.0, 6.0, ((0, 4), (1, 64)), jnp.float32),
        "window_slots": draw_window_slots(jax.random.fold_in(key_list[7], 71), 0),
        "edge_weights": scatter_about(key_list[3], (LAYERS, BLOCKS, FANOUT, BLOCK, BLOCK), (4 * FANOUT * BLOCK) ** -0.5, 0.125, ((1, 64),)),
        "inner_weight": scatter_about(key_list[4], (LAYERS, D, HID), D ** -0.5, 0.375),
        "inner_bias": scatter_about(key_list[5], (LAYERS, HID), 1.0, 5.0, (), jnp.float32),
        "outer_weight": scatter_about(key_list[6], (LAYERS, HID, D), HID ** -0.5, 0.1875),
    }


HALF_ROOT = 0.7071067811865476
DENSITY_NORM = 0.3989422804014327


def smooth_gate(values):
    return 0.5 * values * (1.0 + lax.erf(values * HALF_ROOT))


def smooth_slope(values):
    return 0.5 * (1.0 + lax.erf(values * HALF_ROOT)) + values * jnp.exp(-0.5 * values * values) * DENSITY_NORM


def block_targets(window_slots):
    block_count = window_slots.shape[0]
    block_ids = jnp.arange(block_count, dtype=jnp.int32)
    first_block = block_ids - block_ids % BLK_DEV
    return jnp.mod(first_block[:, None] + window_slots - 1, block_count).astype(jnp.int32)


def aggregate(source, targets, weights):
    block_view = source.astype(jnp.float32).reshape(BLOCKS, BLOCK, D)
    accumulated = jnp.zeros((BLOCKS, BLOCK, D), jnp.float32)
    for column in range(FANOUT):
        picked = block_view[targets[:, column]]
        accumulated = accumulated + jnp.einsum("bmn,bnd->bmd", weights[:, column].astype(jnp.float32), picked, precision=lax.Precision.HIGHEST)
    return accumulated.reshape(NODES, D)


def transpose_aggregate(source, targets, weights):
    block_view = source.astype(jnp.float32).reshape(BLOCKS, BLOCK, D)
    accumulated = jnp.zeros((BLOCKS, BLOCK, D), jnp.float32)
    for column in range(FANOUT):
        pieces = jnp.einsum("bmn,bmd->bnd", weights[:, column].astype(jnp.float32), block_view, precision=lax.Precision.HIGHEST)
        accumulated = accumulated + jax.ops.segment_sum(pieces, targets[:, column], num_segments=BLOCKS)
    return accumulated.reshape(NODES, D)


def linearize(state, targets, edge_weights, inner_weight, inner_bias, outer_weight):
    base_state = state
    slopes = []
    for layer_index in range(LAYERS):
        base_sum = base_state.astype(jnp.float32) + aggregate(base_state, targets, edge_weights[layer_index])
        activation = jnp.dot(base_sum.astype(jnp.bfloat16), inner_weight[layer_index], preferred_element_type=jnp.float32) + inner_bias[layer_index]
        slopes.append(smooth_slope(activation))
        if layer_index + 1 < LAYERS:
            gated = smooth_gate(activation).astype(jnp.bfloat16)
            base_state = (base_sum + jnp.dot(gated, outer_weight[layer_index], preferred_element_type=jnp.float32)).astype(jnp.bfloat16)
    return slopes


def reference(states, increment, window_slots, edge_weights, inner_weight, inner_bias, outer_weight):
    targets = block_targets(window_slots)

    def forward_one(stacked):
        state, source = stacked
        slopes = linearize(state, targets, edge_weights, inner_weight, inner_bias, outer_weight)
        tangent = source
        for layer_index in range(LAYERS):
            tangent_sum = tangent + aggregate(tangent.astype(jnp.bfloat16), targets, edge_weights[layer_index])
            lifted = (slopes[layer_index] * jnp.dot(tangent_sum.astype(jnp.bfloat16), inner_weight[layer_index], preferred_element_type=jnp.float32)).astype(jnp.bfloat16)
            tangent = tangent_sum + jnp.dot(lifted, outer_weight[layer_index], preferred_element_type=jnp.float32)
        return tangent

    images = lax.map(forward_one, (states, increment))
    misfit = jnp.concatenate([increment[:1], increment[1:] - images[:-1]], axis=0)
    following = jnp.concatenate([misfit[1:], jnp.zeros_like(misfit[:1])], axis=0)

    def adjoint_one(stacked):
        state, cotangent = stacked
        slopes = linearize(state, targets, edge_weights, inner_weight, inner_bias, outer_weight)
        current = cotangent
        for layer_index in range(LAYERS - 1, -1, -1):
            narrow = current.astype(jnp.bfloat16)
            spread = jnp.dot(narrow, outer_weight[layer_index].T, preferred_element_type=jnp.float32)
            pulled = (slopes[layer_index] * spread).astype(jnp.bfloat16)
            returned = current + jnp.dot(pulled, inner_weight[layer_index].T, preferred_element_type=jnp.float32)
            current = returned + transpose_aggregate(returned.astype(jnp.bfloat16), targets, edge_weights[layer_index])
        return current

    pulled_back = lax.map(adjoint_one, (states, following))
    return misfit, misfit - pulled_back
```

```python
import jax
import jax.numpy as jnp
from jax import lax
from jax.experimental import pallas as pl
from jax.experimental.pallas import tpu as pltpu
from jax.sharding import PartitionSpec as P

BF = jnp.bfloat16
F32 = jnp.float32
G = 4
NW = 2
B = 128
D = 256
HID = 1024
HC = 256
TM = 4
PARTS = 64
HALF_ROOT = 0.7071067811865476
DENSITY_NORM = 0.3989422804014327


def dot(a, b, ca=1, cb=0):
    return lax.dot_general(a, b, (((ca,), (cb,)), ((), ())), preferred_element_type=F32)


def origin(y, k):
    return lax.rem(y + G - k, G)


def stack(*values):
    return jnp.concatenate(values, axis=0)


def pack_kernel(info, states, inc, *outs):
    y = info[0]
    for k in range(1, G):
        m = lax.rem(y + k, G)
        for w in range(NW):
            outs[k - 1][w, 0] = states[NW * m + w]
            outs[k - 1][w, 1] = inc[NW * m + w].astype(BF)


def fold_kernel(info, slots, states, inc, edges, own, a0, *ext):
    y = info[0]
    for w in range(NW):
        own[w, 0] = states[NW * y + w]
        own[w, 1] = inc[NW * y + w].astype(BF)
    for layer in range(2):
        for slot in range(3):
            total = jnp.zeros((B, B), F32)
            for f in range(4):
                total += jnp.where(slots[0, f] == slot, edges[layer, 0, f].astype(F32), 0.0)
            cols = slice(slot * B, (slot + 1) * B)
            if layer == 0:
                a0[:, cols] = total.astype(BF)
            else:
                for k in range(G):
                    ext[k][:, cols] = total.astype(BF)
    for k in range(G):
        m = lax.rem(y + k + 1, G)
        ext[k][:, 3 * B :] = inc[NW * m].astype(BF)


def edge_kernel(info, r0, r1, r2, r3, send_left, send_right, sems):
    y = info[0]
    for k, r in enumerate((r0, r1, r2, r3)):
        block = origin(y, k)

        @pl.when(block == 0)
        def _():
            pltpu.make_async_copy(r, send_left, sems.at[0]).start()

        @pl.when(block == G - 1)
        def _():
            pltpu.make_async_copy(r, send_right, sems.at[1]).start()

    pltpu.make_async_copy(r0, send_left, sems.at[0]).wait()
    pltpu.make_async_copy(r0, send_right, sems.at[1]).wait()


def sort_edges(y, mats, amat, tmat):
    for k, a in enumerate(mats):
        amat[origin(y, k)] = a[:, : 3 * B]
    for c in range(G):
        for slot in range(3):
            t = jnp.transpose(amat[c, :, slot * B : (slot + 1) * B].astype(F32)).astype(BF)
            to = c + slot - 1
            if 0 <= to < G:
                place = 2 - slot
            else:
                to, place = c, slot
            tmat[to, :, place * B : (place + 1) * B] = t


def pair_matrix(mats, hat):
    hat[0:B, 3 * B :] = jnp.zeros((B, B), BF)
    hat[B:, 0:B] = jnp.zeros((B, B), BF)
    hat[0:B, 0 : 3 * B] = mats[1]
    hat[B:, B:] = mats[2]


def forward_rows(base_sum, tan_sum, win, bias, wout, slope, with_base):
    both = stack(base_sum.astype(BF), tan_sum.astype(BF))
    half = base_sum.shape[0]
    for h in range(HID // HC):
        cols = slice(h * HC, (h + 1) * HC)
        z = dot(both, win[:, cols])
        act = z[:half] + bias[:, cols]
        phi = 0.5 * (1.0 + lax.erf(act * HALF_ROOT))
        slp = phi + act * jnp.exp(-0.5 * act * act) * DENSITY_NORM
        slope[:, cols] = slp.astype(BF)
        lifted = (slp * z[half:]).astype(BF)
        tan_sum = tan_sum + dot(lifted, wout[cols, :])
        if with_base:
            base_sum = base_sum + dot((act * phi).astype(BF), wout[cols, :])
    return base_sum, tan_sum


def adjoint_rows(current, win, wout, slope):
    narrow = current.astype(BF)
    for h in range(HID // HC):
        cols = slice(h * HC, (h + 1) * HC)
        up = dot(narrow, wout[cols, :], 1, 1)
        pulled = (slope[:, cols].astype(F32) * up).astype(BF)
        current = current + dot(pulled, win[:, cols], 1, 1)
    return current


def inner0_kernel(
    info, r0, r1, r2, r3, a0, a1, a2, a3, win, bias, wout,
    field, amat, tmat, base_out, tan_out, slope, hat,
):
    y = info[0]
    sort_edges(y, (a0, a1, a2, a3), amat, tmat)
    pair_matrix(amat, hat)
    for k, r in enumerate((r0, r1, r2, r3)):
        block = origin(y, k)
        rows = pl.ds(pl.multiple_of(block * B, B), B)
        for w in range(NW):
            field[w, rows, 0:D] = r[w, 0]
            field[w, rows, D:] = r[w, 1]
    for w in range(NW):
        agg = dot(hat[...], field[w])
        base_sum = field[w, B : 3 * B, 0:D].astype(F32) + agg[:, 0:D]
        tan_sum = field[w, B : 3 * B, D:].astype(F32) + agg[:, D:]
        base, tan = forward_rows(base_sum, tan_sum, win, bias, wout, slope.at[w], True)
        base_out[w] = base.astype(BF)
        tan_out[w] = tan


def edge0_kernel(
    field, amat, left, right, win, bias, wout,
    send_left, send_right, tan_out, slope,
):
    for w in range(NW):
        lo = stack(jnp.concatenate([left[w, 0], left[w, 1]], axis=1), field[w, 0 : 2 * B])
        hi = stack(field[w, 2 * B :], jnp.concatenate([right[w, 0], right[w, 1]], axis=1))
        agg = stack(dot(amat[0], lo), dot(amat[G - 1], hi))
        own = stack(field[w, 0:B], field[w, 3 * B :]).astype(F32)
        base, tan = forward_rows(
            own[:, 0:D] + agg[:, 0:D], own[:, D:] + agg[:, D:], win, bias, wout, slope.at[w], True
        )
        tan_out[w] = tan
        base, tan = base.astype(BF), tan.astype(BF)
        send_left[w, 0] = base[0:B]
        send_left[w, 1] = tan[0:B]
        send_right[w, 0] = base[B:]
        send_right[w, 1] = tan[B:]


def inner1_kernel(
    info, base_in, tan_in, lo, hi, field, e0, e0r, e1, e2, e3, win, bias, wout,
    amat, tmat, next_out, image, returned, hat, slope, nxt,
):
    y = info[0]
    sort_edges(y, (e0, e1, e2, e3), amat, tmat)
    pair_matrix(amat, hat)
    for k, e in enumerate((e0, e1, e2, e3)):
        value = e[:, 3 * B :]
        if k == 0:
            value = jnp.where(y == G - 1, e0r[:, 3 * B :], value)
        nxt[origin(y, k)] = value
    next_out[0:B] = nxt[0]
    next_out[B:] = nxt[G - 1]
    for w in range(NW):
        base = stack(lo[w, 0], base_in[w], hi[w, 0])
        tan = stack(lo[w, 1], tan_in[w].astype(BF), hi[w, 1])
        base_sum = base_in[w].astype(F32) + dot(hat[...], base)
        tan_sum = tan_in[w] + dot(hat[...], tan)
        _, out = forward_rows(base_sum, tan_sum, win, bias, wout, slope, False)
        image[w] = out.astype(BF)
        if w == 0:
            following = field[1, B : 3 * B, D:].astype(F32)
            current = following - out
        else:
            following = stack(nxt[1], nxt[2]).astype(F32)
            current = jnp.where(info[1] == 1, 0.0, following - out)
        returned[w] = adjoint_rows(current, win, wout, slope)


def edge1_kernel(
    info, lo, hi, tan_edge, base_in, tan_in, left, right, field, next_edge, amat, tmat, image_in, win, bias, wout,
    im0, im1, im2, im3, returned, send_left, send_right, slope, image,
):
    y = info[0]
    for w in range(NW):
        tan_mid = tan_in[w].astype(BF)
        agg = []
        for f, mid in ((0, base_in[w]), (1, tan_mid)):
            agg.append(stack(
                dot(amat[0], stack(left[w, f], lo[w, f], mid[0:B])),
                dot(amat[G - 1], stack(mid[B:], hi[w, f], right[w, f])),
            ))
        base_sum = stack(lo[w, 0], hi[w, 0]).astype(F32) + agg[0]
        _, out = forward_rows(base_sum, tan_edge[w] + agg[1], win, bias, wout, slope, False)
        image[0, w] = out[0:B].astype(BF)
        image[1, w] = image_in[w, 0:B]
        image[2, w] = image_in[w, B:]
        image[3, w] = out[B:].astype(BF)
        if w == 0:
            following = stack(field[1, 0:B, D:], field[1, 3 * B :, D:]).astype(F32)
            current = following - out
        else:
            current = jnp.where(info[1] == 1, 0.0, next_edge[...].astype(F32) - out)
        back = adjoint_rows(current, win, wout, slope)
        returned[w] = back
        send_left[w] = dot(tmat[0, :, 0:B], back[0:B].astype(BF)).astype(BF)
        send_right[w] = dot(tmat[G - 1, :, 2 * B :], back[B:].astype(BF)).astype(BF)
    for k, im in enumerate((im0, im1, im2, im3)):
        im[...] = image[lax.rem(y + k, G)]


def spread_edge(tmat, edge, narrow):
    return edge + stack(
        dot(tmat[0, :, B:], narrow[0 : 2 * B]), dot(tmat[G - 1, :, 0 : 2 * B], narrow[2 * B :])
    )


def inner2_kernel(inner, edge, tmat, slope, win, wout, cur_edge, returned, hat):
    pair_matrix(tmat, hat)
    for w in range(NW):
        narrow = stack(edge[w, 0:B], inner[w], edge[w, B:]).astype(BF)
        cur_edge[w] = spread_edge(tmat, edge[w], narrow)
        current = inner[w] + dot(hat[...], narrow)
        returned[w] = adjoint_rows(current, win, wout, slope.at[w])


def edge2_kernel(cur_edge, left, right, tmat, slope, win, wout, returned, send_left, send_right):
    for w in range(NW):
        current = cur_edge[w] + stack(left[w], right[w]).astype(F32)
        back = adjoint_rows(current, win, wout, slope.at[w])
        returned[w] = back
        send_left[w] = dot(tmat[0, :, 0:B], back[0:B].astype(BF)).astype(BF)
        send_right[w] = dot(tmat[G - 1, :, 2 * B :], back[B:].astype(BF)).astype(BF)


def inner3_kernel(inner, edge, tmat, cur_edge, cur_inner, hat):
    pair_matrix(tmat, hat)
    for w in range(NW):
        narrow = stack(edge[w, 0:B], inner[w], edge[w, B:]).astype(BF)
        cur_edge[w] = spread_edge(tmat, edge[w], narrow)
        cur_inner[w] = (inner[w] + dot(hat[...], narrow)).astype(BF)


def finish_kernel(info, cur_edge, cur_inner, left, right, o0, o1, o2, o3, all_blocks):
    y = info[0]
    for w in range(NW):
        all_blocks[0, w] = (cur_edge[w, 0:B] + left[w].astype(F32)).astype(BF)
        all_blocks[1, w] = cur_inner[w, 0:B]
        all_blocks[2, w] = cur_inner[w, B:]
        all_blocks[3, w] = (cur_edge[w, B:] + right[w].astype(F32)).astype(BF)
    for k, out in enumerate((o0, o1, o2, o3)):
        out[...] = all_blocks[lax.rem(y + k, G)]


def last_image_kernel(info, i0, i1, i2, i3, out, sem):
    y = info[0]
    for k, im in enumerate((i0, i1, i2, i3)):

        @pl.when(origin(y, k) == G - 1)
        def _():
            pltpu.make_async_copy(im.at[NW - 1], out, sem).start()

    pltpu.make_async_copy(i0.at[NW - 1], out, sem).wait()


def misfit_kernel(info, inc, i0, i1, i2, i3, before, misfit):
    y = info[0]
    for k, im in enumerate((i0, i1, i2, i3)):
        m = origin(y, k)
        misfit[NW * m + 1] = inc[NW * m + 1] - im[0].astype(F32)
        even = NW * lax.rem(m + 1, G)
        image = jnp.where(m == G - 1, before[...], im[1])
        misfit[even] = inc[even] - image.astype(F32)


def normal_kernel(info, misfit, p0, p1, p2, p3, normal):
    y = info[0]
    for k, part in enumerate((p0, p1, p2, p3)):
        m = origin(y, k)
        for w in range(NW):
            normal[NW * m + w] = misfit[NW * m + w] - part[w].astype(F32)


SMEM = pl.BlockSpec(memory_space=pltpu.SMEM)
VMEM = pl.BlockSpec(memory_space=pltpu.VMEM)
ANY = pl.BlockSpec(memory_space=pl.ANY)


def sds(shape, dtype=BF):
    return jax.ShapeDtypeStruct(shape, dtype)


def call(kernel, name, ins, outs, scratch=(), smem=0, layers=(), space=VMEM):
    specs = [SMEM] * smem + [space] * (len(ins) - smem)
    for position, layer in layers:
        shape = ins[position].shape
        specs[position] = pl.BlockSpec((None,) + shape[1:], lambda i, layer=layer: (layer, 0, 0))
    return pl.pallas_call(
        kernel,
        name=name,
        grid=(1,),
        out_shape=outs,
        in_specs=specs,
        out_specs=[space] * len(outs),
        scratch_shapes=list(scratch),
        compiler_params=pltpu.CompilerParams(vmem_limit_bytes=60 * 1024 * 1024),
    )(*ins)


def group_pairs(k):
    return [(b, b // G * G + (b + k) % G) for b in range(PARTS)]


def side_pairs(d):
    return [(b, (b + G * d) % PARTS) for b in range(PARTS)]


def next_increment_pairs(k):
    pairs = []
    for t in range(TM):
        for b in range(PARTS):
            m = (b + k) % G
            if k == 0 and m != G - 1:
                continue
            to = (t - 1) % TM if m == G - 1 else t
            pairs.append((t * PARTS + b, to * PARTS + b // G * G + m))
    return pairs


def to_members(sends):
    return [sends[0]] + [lax.ppermute(sends[k], "mesh", group_pairs(k)) for k in range(1, G)]


def swap_sides(send_left, send_right):
    left = lax.ppermute(send_right, "mesh", side_pairs(1))
    right = lax.ppermute(send_left, "mesh", side_pairs(-1))
    return left, right


def local(states, increment, window_slots, edge_weights, inner_weight, inner_bias, outer_weight):
    y = lax.rem(lax.axis_index("mesh"), G).astype(jnp.int32)
    ends = jnp.logical_and(y == G - 1, lax.axis_index("tm") == TM - 1).astype(jnp.int32)
    info = jnp.stack([y, ends])
    bias = inner_bias.reshape(2, 1, HID)

    item = sds((NW, 2, B, D))
    half = sds((NW, B, D))
    pair_bf = sds((NW, 2 * B, D))
    pair = sds((NW, 2 * B, D), F32)
    hidden = sds((NW, 2 * B, HID))
    mats = sds((G, B, 3 * B))
    hat = pltpu.VMEM((2 * B, 4 * B), BF)
    dma = pltpu.SemaphoreType.DMA

    sends = call(pack_kernel, "pack", (info, states, increment), [item] * (G - 1), smem=1)
    own, a0, *ext = call(
        fold_kernel, "fold", (info, window_slots, states, increment, edge_weights),
        [item, sds((B, 3 * B))] + [sds((B, 3 * B + D))] * G, smem=2,
    )
    got = to_members([own, *sends])
    a0 = to_members([a0] * G)
    moved = [lax.ppermute(ext[k], ("tm", "mesh"), next_increment_pairs(k)) for k in range(G)]

    lo, hi = call(
        edge_kernel, "edge", (info, *got), [item, item], (dma((2,)),), smem=1, space=ANY,
    )
    left, right = swap_sides(lo, hi)
    field, amat0, tmat0, base_in, tan_in, slope_in = call(
        inner0_kernel, "inner0", (info, *got, *a0, inner_weight, bias, outer_weight),
        [sds((NW, G * B, 2 * D)), mats, mats, pair_bf, pair, hidden],
        (hat,), smem=1, layers=((9, 0), (10, 0), (11, 0)),
    )
    lo, hi, tan_edge, slope_edge = call(
        edge0_kernel, "edge0", (field, amat0, left, right, inner_weight, bias, outer_weight),
        [item, item, pair, hidden], layers=((4, 0), (5, 0), (6, 0)),
    )

    left, right = swap_sides(lo, hi)
    slope1 = pltpu.VMEM((2 * B, HID), BF)
    amat1, tmat1, next_edge, image_in, inner = call(
        inner1_kernel, "inner1",
        (info, base_in, tan_in, lo, hi, field, ext[0], *moved, inner_weight, bias, outer_weight),
        [mats, mats, sds((2 * B, D)), pair_bf, pair],
        (hat, slope1, pltpu.VMEM((G, B, D), BF)), smem=1, layers=((11, 1), (12, 1), (13, 1)),
    )
    *images, edge, send_left, send_right = call(
        edge1_kernel, "edge1",
        (info, lo, hi, tan_edge, base_in, tan_in, left, right, field, next_edge, amat1, tmat1, image_in,
         inner_weight, bias, outer_weight),
        [half] * G + [pair, half, half],
        (slope1, pltpu.VMEM((G, NW, B, D), BF)), smem=1, layers=((13, 1), (14, 1), (15, 1)),
    )

    left, right = swap_sides(send_left, send_right)
    images = to_members(images)
    cur_edge, inner = call(
        inner2_kernel, "inner2", (inner, edge, tmat1, slope_in, inner_weight, outer_weight),
        [pair, pair], (hat,), layers=((4, 0), (5, 0)),
    )
    edge, send_left, send_right = call(
        edge2_kernel, "edge2", (cur_edge, left, right, tmat0, slope_edge, inner_weight, outer_weight),
        [pair, half, half], layers=((5, 0), (6, 0)),
    )

    left, right = swap_sides(send_left, send_right)
    (last,) = call(
        last_image_kernel, "last_image", (info, *images), [sds((B, D))], (dma,), smem=1, space=ANY,
    )
    before = lax.ppermute(last, "tm", [(t, t + 1) for t in range(TM - 1)])
    cur_edge, cur_inner = call(
        inner3_kernel, "inner3", (inner, edge, tmat0), [pair, pair_bf], (hat,),
    )
    parts = call(
        finish_kernel, "finish", (info, cur_edge, cur_inner, left, right), [half] * G,
        (pltpu.VMEM((G, NW, B, D), BF),), smem=1,
    )
    parts = to_members(parts)
    whole = sds(increment.shape, F32)
    (misfit,) = call(misfit_kernel, "misfit", (info, increment, *images, before), [whole], smem=1)
    (normal,) = call(normal_kernel, "normal", (info, misfit, *parts), [whole], smem=1)
    return misfit, normal


def solution(mesh):
    placed = (
        P("tm", "mesh", None),
        P("tm", "mesh", None),
        P("mesh", None),
        P(None, "mesh", None, None, None),
        P(),
        P(),
        P(),
    )
    return jax.shard_map(
        local,
        mesh=mesh,
        in_specs=placed,
        out_specs=(P("tm", "mesh", None), P("tm", "mesh", None)),
        check_vma=False,
    )
```

```python
import jax
import jax.numpy as jnp
from jax import lax
from jax.experimental import pallas as pl
from jax.experimental.pallas import tpu as pltpu
from jax.sharding import PartitionSpec as P


BF = jnp.bfloat16
F32 = jnp.float32
G = 4
NW = 2
B = 128
D = 256
HID = 1024
HC = 256
TM = 4
PARTS = 64
HALF_ROOT = 0.7071067811865476
DENSITY_NORM = 0.3989422804014327


def dot(a, b, ca=1, cb=0):
    return lax.dot_general(a, b, (((ca,), (cb,)), ((), ())), preferred_element_type=F32)


def member():
    return lax.rem(lax.axis_index("mesh"), G)


def last_member():
    return jnp.logical_and(member() == G - 1, lax.axis_index("tm") == TM - 1)


def origin(y, k):
    return lax.rem(y + G - k, G)


def stack(*values):
    return jnp.concatenate(values, axis=0)


def pack_kernel(states, inc, *outs):
    y = member()
    for k in range(1, G):
        m = lax.rem(y + k, G)
        for w in range(NW):
            outs[k - 1][w, 0] = states[NW * m + w]
            outs[k - 1][w, 1] = inc[NW * m + w].astype(BF)


def fold_kernel(slots, states, inc, edges, own, cross, *ext):
    y = member()
    for w in range(NW):
        own[w, 0] = states[NW * y + w]
        own[w, 1] = inc[NW * y + w].astype(BF)
    for layer in range(2):
        for slot in range(3):
            total = jnp.zeros((B, B), F32)
            for f in range(4):
                total += jnp.where(slots[0, f] == slot, edges[layer, 0, f].astype(F32), 0.0)
            first = (3 * layer + slot) * B
            for k in range(G):
                ext[k][:, first : first + B] = total.astype(BF)
    for k in range(G):
        m = lax.rem(y + k + 1, G)
        value = inc[NW * m].astype(BF)
        ext[k][:, 6 * B :] = value
        if k == 0:
            cross[...] = value


def edge_kernel(r0, r1, r2, r3, send_left, send_right):
    y = member()
    for k, r in enumerate((r0, r1, r2, r3)):
        block = origin(y, k)

        @pl.when(block == 0)
        def _():
            send_left[...] = r[...]

        @pl.when(block == G - 1)
        def _():
            send_right[...] = r[...]


def sort_edges(y, mats, first, amat, tmat):
    for k, a in enumerate(mats):
        amat[origin(y, k)] = a[:, first : first + 3 * B]
    for c in range(G):
        for slot in range(3):
            t = jnp.transpose(amat[c, :, slot * B : (slot + 1) * B].astype(F32)).astype(BF)
            to = c + slot - 1
            if 0 <= to < G:
                place = 2 - slot
            else:
                to, place = c, slot
            tmat[to, :, place * B : (place + 1) * B] = t


def pair_matrix(mats, hat):
    hat[0:B, 3 * B :] = jnp.zeros((B, B), BF)
    hat[B:, 0:B] = jnp.zeros((B, B), BF)
    hat[0:B, 0 : 3 * B] = mats[1]
    hat[B:, B:] = mats[2]


def forward_rows(base_sum, tan_sum, layer, win, bias, wout, slope, with_base):
    both = stack(base_sum.astype(BF), tan_sum.astype(BF))
    half = base_sum.shape[0]
    for h in range(HID // HC):
        cols = slice(h * HC, (h + 1) * HC)
        z = dot(both, win[:, cols])
        act = z[:half] + bias[layer : layer + 1, cols]
        phi = 0.5 * (1.0 + lax.erf(act * HALF_ROOT))
        slp = phi + act * jnp.exp(-0.5 * act * act) * DENSITY_NORM
        slope[:, cols] = slp.astype(BF)
        lifted = (slp * z[half:]).astype(BF)
        tan_sum = tan_sum + dot(lifted, wout[cols, :])
        if with_base:
            base_sum = base_sum + dot((act * phi).astype(BF), wout[cols, :])
    return base_sum, tan_sum


def adjoint_rows(current, win, wout, slope):
    narrow = current.astype(BF)
    for h in range(HID // HC):
        cols = slice(h * HC, (h + 1) * HC)
        up = dot(narrow, wout[cols, :], 1, 1)
        pulled = (slope[:, cols].astype(F32) * up).astype(BF)
        current = current + dot(pulled, win[:, cols], 1, 1)
    return current


def inner0_kernel(
    r0, r1, r2, r3, a0, a1, a2, a3, win, bias, wout,
    field, amat, tmat, base_out, tan_out, slope, hat,
):
    y = member()
    sort_edges(y, (a0, a1, a2, a3), 0, amat, tmat)
    pair_matrix(amat, hat)
    for k, r in enumerate((r0, r1, r2, r3)):
        block = origin(y, k)
        rows = pl.ds(pl.multiple_of(block * B, B), B)
        for w in range(NW):
            field[w, rows, 0:D] = r[w, 0]
            field[w, rows, D:] = r[w, 1]
    for w in range(NW):
        agg = dot(hat[...], field[w])
        base_sum = field[w, B : 3 * B, 0:D].astype(F32) + agg[:, 0:D]
        tan_sum = field[w, B : 3 * B, D:].astype(F32) + agg[:, D:]
        base, tan = forward_rows(base_sum, tan_sum, 0, win, bias, wout, slope.at[w], True)
        base_out[w] = base.astype(BF)
        tan_out[w] = tan


def edge0_kernel(
    field, amat, left, right, win, bias, wout,
    send_left, send_right, tan_out, slope,
):
    for w in range(NW):
        lo = stack(jnp.concatenate([left[w, 0], left[w, 1]], axis=1), field[w, 0 : 2 * B])
        hi = stack(field[w, 2 * B :], jnp.concatenate([right[w, 0], right[w, 1]], axis=1))
        agg = stack(dot(amat[0], lo), dot(amat[G - 1], hi))
        own = stack(field[w, 0:B], field[w, 3 * B :]).astype(F32)
        base, tan = forward_rows(
            own[:, 0:D] + agg[:, 0:D], own[:, D:] + agg[:, D:], 0, win, bias, wout, slope.at[w], True
        )
        tan_out[w] = tan
        base, tan = base.astype(BF), tan.astype(BF)
        send_left[w, 0] = base[0:B]
        send_left[w, 1] = tan[0:B]
        send_right[w, 0] = base[B:]
        send_right[w, 1] = tan[B:]


def inner1_kernel(
    base_in, tan_in, lo, hi, field, e0, e0r, e1, e2, e3, win, bias, wout,
    amat, tmat, next_out, image, returned, hat, slope, nxt,
):
    y = member()
    sort_edges(y, (e0, e1, e2, e3), 3 * B, amat, tmat)
    pair_matrix(amat, hat)
    for k, e in enumerate((e0, e1, e2, e3)):
        value = e[:, 6 * B :]
        if k == 0:
            value = jnp.where(y == G - 1, e0r[...], value)
        nxt[origin(y, k)] = value
    next_out[0:B] = nxt[0]
    next_out[B:] = nxt[G - 1]
    for w in range(NW):
        base = stack(lo[w, 0], base_in[w], hi[w, 0])
        tan = stack(lo[w, 1], tan_in[w].astype(BF), hi[w, 1])
        base_sum = base_in[w].astype(F32) + dot(hat[...], base)
        tan_sum = tan_in[w] + dot(hat[...], tan)
        _, out = forward_rows(base_sum, tan_sum, 1, win, bias, wout, slope, False)
        image[w] = out.astype(BF)
        if w == 0:
            following = field[1, B : 3 * B, D:].astype(F32)
            current = following - out
        else:
            following = stack(nxt[1], nxt[2]).astype(F32)
            current = jnp.where(last_member(), 0.0, following - out)
        returned[w] = adjoint_rows(current, win, wout, slope)


def edge1_kernel(
    lo, hi, tan_edge, base_in, tan_in, left, right, field, next_edge, amat, tmat, image_in, win, bias, wout,
    im0, im1, im2, im3, returned, send_left, send_right, slope, image,
):
    y = member()
    for w in range(NW):
        tan_mid = tan_in[w].astype(BF)
        agg = []
        for f, mid in ((0, base_in[w]), (1, tan_mid)):
            agg.append(stack(
                dot(amat[0], stack(left[w, f], lo[w, f], mid[0:B])),
                dot(amat[G - 1], stack(mid[B:], hi[w, f], right[w, f])),
            ))
        base_sum = stack(lo[w, 0], hi[w, 0]).astype(F32) + agg[0]
        _, out = forward_rows(base_sum, tan_edge[w] + agg[1], 1, win, bias, wout, slope, False)
        image[0, w] = out[0:B].astype(BF)
        image[1, w] = image_in[w, 0:B]
        image[2, w] = image_in[w, B:]
        image[3, w] = out[B:].astype(BF)
        if w == 0:
            following = stack(field[1, 0:B, D:], field[1, 3 * B :, D:]).astype(F32)
            current = following - out
        else:
            current = jnp.where(last_member(), 0.0, next_edge[...].astype(F32) - out)
        back = adjoint_rows(current, win, wout, slope)
        returned[w] = back
        send_left[w] = dot(tmat[0, :, 0:B], back[0:B].astype(BF)).astype(BF)
        send_right[w] = dot(tmat[G - 1, :, 2 * B :], back[B:].astype(BF)).astype(BF)
    for k, im in enumerate((im0, im1, im2, im3)):
        im[...] = image[lax.rem(y + k, G)]


def spread_edge(tmat, edge, narrow):
    return edge + stack(
        dot(tmat[0, :, B:], narrow[0 : 2 * B]), dot(tmat[G - 1, :, 0 : 2 * B], narrow[2 * B :])
    )


def inner2_kernel(inner, edge, tmat, slope, win, wout, cur_edge, returned, hat):
    pair_matrix(tmat, hat)
    for w in range(NW):
        narrow = stack(edge[w, 0:B], inner[w], edge[w, B:]).astype(BF)
        cur_edge[w] = spread_edge(tmat, edge[w], narrow)
        current = inner[w] + dot(hat[...], narrow)
        returned[w] = adjoint_rows(current, win, wout, slope.at[w])


def edge2_kernel(cur_edge, left, right, tmat, slope, win, wout, returned, send_left, send_right):
    for w in range(NW):
        current = cur_edge[w] + stack(left[w], right[w]).astype(F32)
        back = adjoint_rows(current, win, wout, slope.at[w])
        returned[w] = back
        send_left[w] = dot(tmat[0, :, 0:B], back[0:B].astype(BF)).astype(BF)
        send_right[w] = dot(tmat[G - 1, :, 2 * B :], back[B:].astype(BF)).astype(BF)


def inner3_kernel(inner, edge, tmat, i0, i1, i2, i3, cur_edge, cur_inner, last, hat):
    y = member()
    for k, im in enumerate((i0, i1, i2, i3)):

        @pl.when(origin(y, k) == G - 1)
        def _():
            last[...] = im[NW - 1]

    pair_matrix(tmat, hat)
    for w in range(NW):
        narrow = stack(edge[w, 0:B], inner[w], edge[w, B:]).astype(BF)
        cur_edge[w] = spread_edge(tmat, edge[w], narrow)
        cur_inner[w] = (inner[w] + dot(hat[...], narrow)).astype(BF)


def finish_kernel(cur_edge, cur_inner, left, right, o0, o1, o2, o3, all_blocks):
    y = member()
    for w in range(NW):
        all_blocks[0, w] = (cur_edge[w, 0:B] + left[w].astype(F32)).astype(BF)
        all_blocks[1, w] = cur_inner[w, 0:B]
        all_blocks[2, w] = cur_inner[w, B:]
        all_blocks[3, w] = (cur_edge[w, B:] + right[w].astype(F32)).astype(BF)
    for k, out in enumerate((o0, o1, o2, o3)):
        out[...] = all_blocks[lax.rem(y + k, G)]


def misfit_kernel(inc, i0, i1, i2, i3, before, misfit):
    y = member()
    for k, im in enumerate((i0, i1, i2, i3)):
        m = origin(y, k)
        misfit[NW * m + 1] = inc[NW * m + 1] - im[0].astype(F32)
        even = NW * lax.rem(m + 1, G)
        image = jnp.where(m == G - 1, before[...], im[1])
        misfit[even] = inc[even] - image.astype(F32)


def normal_kernel(misfit, p0, p1, p2, p3, normal):
    y = member()
    for k, part in enumerate((p0, p1, p2, p3)):
        m = origin(y, k)
        for w in range(NW):
            normal[NW * m + w] = misfit[NW * m + w] - part[w].astype(F32)


SMEM = pl.BlockSpec(memory_space=pltpu.SMEM)
VMEM = pl.BlockSpec(memory_space=pltpu.VMEM)


def sds(shape, dtype=BF):
    return jax.ShapeDtypeStruct(shape, dtype)


def call(kernel, ins, outs, scratch=(), smem=0, layer=0, weights=()):
    specs = [SMEM] * smem + [VMEM] * (len(ins) - smem)
    for position in weights:
        shape = ins[position].shape
        specs[position] = pl.BlockSpec((None,) + shape[1:], lambda i: (layer, 0, 0))
    return pl.pallas_call(
        kernel,
        grid=(1,),
        out_shape=outs,
        in_specs=specs,
        out_specs=[VMEM] * len(outs),
        scratch_shapes=list(scratch),
        compiler_params=pltpu.CompilerParams(vmem_limit_bytes=60 * 1024 * 1024),
    )(*ins)


def group_pairs(k):
    return [(b, b // G * G + (b + k) % G) for b in range(PARTS)]


def side_pairs(d):
    return [(b, (b + G * d) % PARTS) for b in range(PARTS)]


def next_increment_pairs(k):
    pairs = []
    for t in range(TM):
        for b in range(PARTS):
            m = (b + k) % G
            if k == 0 and m != G - 1:
                continue
            to = (t - 1) % TM if m == G - 1 else t
            pairs.append((t * PARTS + b, to * PARTS + b // G * G + m))
    return pairs


def to_members(sends):
    return [lax.ppermute(sends[k], "mesh", group_pairs(k)) for k in range(1, G)]


def swap_sides(send_left, send_right):
    left = lax.ppermute(send_right, "mesh", side_pairs(1))
    right = lax.ppermute(send_left, "mesh", side_pairs(-1))
    return left, right


def local(states, increment, window_slots, edge_weights, inner_weight, inner_bias, outer_weight):
    bias = inner_bias

    item = sds((NW, 2, B, D))
    half = sds((NW, B, D))
    pair_bf = sds((NW, 2 * B, D))
    pair = sds((NW, 2 * B, D), F32)
    hidden = sds((NW, 2 * B, HID))
    mats = sds((G, B, 3 * B))
    hat = pltpu.VMEM((2 * B, 4 * B), BF)

    sends = call(pack_kernel, (states, increment), [item] * (G - 1))
    got = [None, *to_members([None, *sends])]
    got[0], cross, *ext = call(
        fold_kernel, (window_slots, states, increment, edge_weights),
        [item, sds((B, D))] + [sds((B, 6 * B + D))] * G, smem=1,
    )
    cross = lax.ppermute(cross, ("tm", "mesh"), next_increment_pairs(0))
    ext = [ext[0]] + [lax.ppermute(ext[k], ("tm", "mesh"), next_increment_pairs(k)) for k in range(1, G)]

    lo, hi = call(edge_kernel, got, [item, item])
    left, right = swap_sides(lo, hi)
    field, amat0, tmat0, base_in, tan_in, slope_in = call(
        inner0_kernel, (*got, *ext, inner_weight, bias, outer_weight),
        [sds((NW, G * B, 2 * D)), mats, mats, pair_bf, pair, hidden], (hat,), weights=(8, 10),
    )
    lo, hi, tan_edge, slope_edge = call(
        edge0_kernel, (field, amat0, left, right, inner_weight, bias, outer_weight),
        [item, item, pair, hidden], weights=(4, 6),
    )

    left, right = swap_sides(lo, hi)
    slope1 = pltpu.VMEM((2 * B, HID), BF)
    amat1, tmat1, next_edge, image_in, inner = call(
        inner1_kernel,
        (base_in, tan_in, lo, hi, field, ext[0], cross, *ext[1:], inner_weight, bias, outer_weight),
        [mats, mats, sds((2 * B, D)), pair_bf, pair],
        (hat, slope1, pltpu.VMEM((G, B, D), BF)), layer=1, weights=(10, 12),
    )
    *images, edge, send_left, send_right = call(
        edge1_kernel,
        (lo, hi, tan_edge, base_in, tan_in, left, right, field, next_edge, amat1, tmat1, image_in,
         inner_weight, bias, outer_weight),
        [half] * G + [pair, half, half],
        (slope1, pltpu.VMEM((G, NW, B, D), BF)), layer=1, weights=(12, 14),
    )

    left, right = swap_sides(send_left, send_right)
    images = [images[0], *to_members(images)]
    cur_edge, inner = call(
        inner2_kernel, (inner, edge, tmat1, slope_in, inner_weight, outer_weight),
        [pair, pair], (hat,), weights=(4, 5),
    )
    edge, send_left, send_right = call(
        edge2_kernel, (cur_edge, left, right, tmat0, slope_edge, inner_weight, outer_weight),
        [pair, half, half], weights=(5, 6),
    )

    left, right = swap_sides(send_left, send_right)
    cur_edge, cur_inner, last = call(
        inner3_kernel, (inner, edge, tmat0, *images), [pair, pair_bf, sds((B, D))], (hat,),
    )
    before = lax.ppermute(last, "tm", [(t, t + 1) for t in range(TM - 1)])
    parts = call(
        finish_kernel, (cur_edge, cur_inner, left, right), [half] * G,
        (pltpu.VMEM((G, NW, B, D), BF),),
    )
    parts = [parts[0], *to_members(parts)]
    whole = sds(increment.shape, F32)
    (misfit,) = call(misfit_kernel, (increment, *images, before), [whole])
    (normal,) = call(normal_kernel, (misfit, *parts), [whole])
    return misfit, normal


def solution(mesh):
    placed = (
        P("tm", "mesh", None),
        P("tm", "mesh", None),
        P("mesh", None),
        P(None, "mesh", None, None, None),
        P(),
        P(),
        P(),
    )

    return jax.shard_map(
        local,
        mesh=mesh,
        in_specs=placed,
        out_specs=(P("tm", "mesh", None), P("tm", "mesh", None)),
        check_vma=False,
    )
```

```python
import jax
import jax.numpy as jnp
from jax import lax
from jax.experimental import pallas as pl
from jax.experimental.pallas import tpu as pltpu
from jax.sharding import PartitionSpec as P


BF = jnp.bfloat16
F32 = jnp.float32
G = 4
NW = 2
B = 128
D = 256
HID = 1024
HC = 256
TM = 4
PARTS = 64
HALF_ROOT = 0.7071067811865476
DENSITY_NORM = 0.3989422804014327


def dot(a, b, ca=1, cb=0):
    return lax.dot_general(a, b, (((ca,), (cb,)), ((), ())), preferred_element_type=F32)


def member():
    return lax.rem(lax.axis_index("mesh"), G)


def last_member():
    return jnp.logical_and(member() == G - 1, lax.axis_index("tm") == TM - 1)


def origin(y, k):
    return lax.rem(y + G - k, G)


def stack(*values):
    return jnp.concatenate(values, axis=0)


def pack_kernel(states, inc, *outs):
    y = member()
    for k in range(1, G):
        m = lax.rem(y + k, G)
        for w in range(NW):
            outs[k - 1][w, 0] = states[NW * m + w]
            outs[k - 1][w, 1] = inc[NW * m + w].astype(BF)


def fold_kernel(slots, states, inc, edges, own, cross, *ext):
    y = member()
    for w in range(NW):
        own[w, 0] = states[NW * y + w]
        own[w, 1] = inc[NW * y + w].astype(BF)
    for layer in range(2):
        for slot in range(3):
            total = jnp.zeros((B, B), F32)
            for f in range(4):
                total += jnp.where(slots[0, f] == slot, edges[layer, 0, f].astype(F32), 0.0)
            first = (3 * layer + slot) * B
            for k in range(G):
                ext[k][:, first : first + B] = total.astype(BF)
    for k in range(G):
        m = lax.rem(y + k + 1, G)
        value = inc[NW * m].astype(BF)
        ext[k][:, 6 * B :] = value
        if k == 0:
            cross[...] = value


def edge_kernel(r0, r1, r2, r3, send_left, send_right):
    y = member()
    for k, r in enumerate((r0, r1, r2, r3)):
        block = origin(y, k)

        @pl.when(block == 0)
        def _():
            send_left[...] = r[...]

        @pl.when(block == G - 1)
        def _():
            send_right[...] = r[...]


def sort_edges(y, mats, first, amat, tmat):
    for k, a in enumerate(mats):
        amat[origin(y, k)] = a[:, first : first + 3 * B]
    for c in range(G):
        for slot in range(3):
            t = jnp.transpose(amat[c, :, slot * B : (slot + 1) * B].astype(F32)).astype(BF)
            to = c + slot - 1
            if 0 <= to < G:
                place = 2 - slot
            else:
                to, place = c, slot
            tmat[to, :, place * B : (place + 1) * B] = t


def pair_matrix(mats, hat):
    hat[0:B, 3 * B :] = jnp.zeros((B, B), BF)
    hat[B:, 0:B] = jnp.zeros((B, B), BF)
    hat[0:B, 0 : 3 * B] = mats[1]
    hat[B:, B:] = mats[2]


def forward_rows(base_sum, tan_sum, layer, win, bias, wout, slope, with_base):
    both = stack(base_sum.astype(BF), tan_sum.astype(BF))
    half = base_sum.shape[0]
    for h in range(HID // HC):
        cols = slice(h * HC, (h + 1) * HC)
        z = dot(both, win[layer, :, cols])
        act = z[:half] + bias[layer : layer + 1, cols]
        phi = 0.5 * (1.0 + lax.erf(act * HALF_ROOT))
        slp = phi + act * jnp.exp(-0.5 * act * act) * DENSITY_NORM
        slope[:, cols] = slp.astype(BF)
        lifted = (slp * z[half:]).astype(BF)
        tan_sum = tan_sum + dot(lifted, wout[layer, cols, :])
        if with_base:
            base_sum = base_sum + dot((act * phi).astype(BF), wout[layer, cols, :])
    return base_sum, tan_sum


def adjoint_rows(current, layer, win, wout, slope):
    narrow = current.astype(BF)
    for h in range(HID // HC):
        cols = slice(h * HC, (h + 1) * HC)
        up = dot(narrow, wout[layer, cols, :], 1, 1)
        pulled = (slope[:, cols].astype(F32) * up).astype(BF)
        current = current + dot(pulled, win[layer, :, cols], 1, 1)
    return current


def inner0_kernel(
    r0, r1, r2, r3, a0, a1, a2, a3, win, bias, wout,
    field, amat, tmat, base_out, tan_out, slope, hat,
):
    y = member()
    sort_edges(y, (a0, a1, a2, a3), 0, amat, tmat)
    pair_matrix(amat, hat)
    for k, r in enumerate((r0, r1, r2, r3)):
        block = origin(y, k)
        rows = pl.ds(pl.multiple_of(block * B, B), B)
        for w in range(NW):
            field[w, rows, 0:D] = r[w, 0]
            field[w, rows, D:] = r[w, 1]
    for w in range(NW):
        agg = dot(hat[...], field[w])
        base_sum = field[w, B : 3 * B, 0:D].astype(F32) + agg[:, 0:D]
        tan_sum = field[w, B : 3 * B, D:].astype(F32) + agg[:, D:]
        base, tan = forward_rows(base_sum, tan_sum, 0, win, bias, wout, slope.at[w], True)
        base_out[w] = base.astype(BF)
        tan_out[w] = tan


def edge0_kernel(
    field, amat, left, right, win, bias, wout,
    send_left, send_right, tan_out, slope,
):
    for w in range(NW):
        lo = stack(jnp.concatenate([left[w, 0], left[w, 1]], axis=1), field[w, 0 : 2 * B])
        hi = stack(field[w, 2 * B :], jnp.concatenate([right[w, 0], right[w, 1]], axis=1))
        agg = stack(dot(amat[0], lo), dot(amat[G - 1], hi))
        own = stack(field[w, 0:B], field[w, 3 * B :]).astype(F32)
        base, tan = forward_rows(
            own[:, 0:D] + agg[:, 0:D], own[:, D:] + agg[:, D:], 0, win, bias, wout, slope.at[w], True
        )
        tan_out[w] = tan
        base, tan = base.astype(BF), tan.astype(BF)
        send_left[w, 0] = base[0:B]
        send_left[w, 1] = tan[0:B]
        send_right[w, 0] = base[B:]
        send_right[w, 1] = tan[B:]


def inner1_kernel(
    base_in, tan_in, lo, hi, field, e0, e0r, e1, e2, e3, win, bias, wout,
    amat, tmat, next_out, image, returned, hat, slope, nxt,
):
    y = member()
    sort_edges(y, (e0, e1, e2, e3), 3 * B, amat, tmat)
    pair_matrix(amat, hat)
    for k, e in enumerate((e0, e1, e2, e3)):
        value = e[:, 6 * B :]
        if k == 0:
            value = jnp.where(y == G - 1, e0r[...], value)
        nxt[origin(y, k)] = value
    next_out[0:B] = nxt[0]
    next_out[B:] = nxt[G - 1]
    for w in range(NW):
        base = stack(lo[w, 0], base_in[w], hi[w, 0])
        tan = stack(lo[w, 1], tan_in[w].astype(BF), hi[w, 1])
        base_sum = base_in[w].astype(F32) + dot(hat[...], base)
        tan_sum = tan_in[w] + dot(hat[...], tan)
        _, out = forward_rows(base_sum, tan_sum, 1, win, bias, wout, slope, False)
        image[w] = out.astype(BF)
        if w == 0:
            following = field[1, B : 3 * B, D:].astype(F32)
            current = following - out
        else:
            following = stack(nxt[1], nxt[2]).astype(F32)
            current = jnp.where(last_member(), 0.0, following - out)
        returned[w] = adjoint_rows(current, 1, win, wout, slope)


def edge1_kernel(
    lo, hi, tan_edge, base_in, tan_in, left, right, field, next_edge, amat, tmat, image_in, win, bias, wout,
    im0, im1, im2, im3, returned, send_left, send_right, slope, image,
):
    y = member()
    for w in range(NW):
        tan_mid = tan_in[w].astype(BF)
        agg = []
        for f, mid in ((0, base_in[w]), (1, tan_mid)):
            agg.append(stack(
                dot(amat[0], stack(left[w, f], lo[w, f], mid[0:B])),
                dot(amat[G - 1], stack(mid[B:], hi[w, f], right[w, f])),
            ))
        base_sum = stack(lo[w, 0], hi[w, 0]).astype(F32) + agg[0]
        _, out = forward_rows(base_sum, tan_edge[w] + agg[1], 1, win, bias, wout, slope, False)
        image[0, w] = out[0:B].astype(BF)
        image[1, w] = image_in[w, 0:B]
        image[2, w] = image_in[w, B:]
        image[3, w] = out[B:].astype(BF)
        if w == 0:
            following = stack(field[1, 0:B, D:], field[1, 3 * B :, D:]).astype(F32)
            current = following - out
        else:
            current = jnp.where(last_member(), 0.0, next_edge[...].astype(F32) - out)
        back = adjoint_rows(current, 1, win, wout, slope)
        returned[w] = back
        send_left[w] = dot(tmat[0, :, 0:B], back[0:B].astype(BF)).astype(BF)
        send_right[w] = dot(tmat[G - 1, :, 2 * B :], back[B:].astype(BF)).astype(BF)
    for k, im in enumerate((im0, im1, im2, im3)):
        im[...] = image[lax.rem(y + k, G)]


def spread_edge(tmat, edge, narrow):
    return edge + stack(
        dot(tmat[0, :, B:], narrow[0 : 2 * B]), dot(tmat[G - 1, :, 0 : 2 * B], narrow[2 * B :])
    )


def inner2_kernel(inner, edge, tmat, slope, win, wout, cur_edge, returned, hat):
    pair_matrix(tmat, hat)
    for w in range(NW):
        narrow = stack(edge[w, 0:B], inner[w], edge[w, B:]).astype(BF)
        cur_edge[w] = spread_edge(tmat, edge[w], narrow)
        current = inner[w] + dot(hat[...], narrow)
        returned[w] = adjoint_rows(current, 0, win, wout, slope.at[w])


def edge2_kernel(cur_edge, left, right, tmat, slope, win, wout, returned, send_left, send_right):
    for w in range(NW):
        current = cur_edge[w] + stack(left[w], right[w]).astype(F32)
        back = adjoint_rows(current, 0, win, wout, slope.at[w])
        returned[w] = back
        send_left[w] = dot(tmat[0, :, 0:B], back[0:B].astype(BF)).astype(BF)
        send_right[w] = dot(tmat[G - 1, :, 2 * B :], back[B:].astype(BF)).astype(BF)


def inner3_kernel(inner, edge, tmat, i0, i1, i2, i3, cur_edge, cur_inner, last, hat):
    y = member()
    for k, im in enumerate((i0, i1, i2, i3)):

        @pl.when(origin(y, k) == G - 1)
        def _():
            last[...] = im[NW - 1]

    pair_matrix(tmat, hat)
    for w in range(NW):
        narrow = stack(edge[w, 0:B], inner[w], edge[w, B:]).astype(BF)
        cur_edge[w] = spread_edge(tmat, edge[w], narrow)
        cur_inner[w] = (inner[w] + dot(hat[...], narrow)).astype(BF)


def finish_kernel(cur_edge, cur_inner, left, right, o0, o1, o2, o3, all_blocks):
    y = member()
    for w in range(NW):
        all_blocks[0, w] = (cur_edge[w, 0:B] + left[w].astype(F32)).astype(BF)
        all_blocks[1, w] = cur_inner[w, 0:B]
        all_blocks[2, w] = cur_inner[w, B:]
        all_blocks[3, w] = (cur_edge[w, B:] + right[w].astype(F32)).astype(BF)
    for k, out in enumerate((o0, o1, o2, o3)):
        out[...] = all_blocks[lax.rem(y + k, G)]


def misfit_kernel(inc, i0, i1, i2, i3, before, misfit, kept):
    y = member()
    for k, im in enumerate((i0, i1, i2, i3)):
        m = origin(y, k)
        value = inc[NW * m + 1] - im[0].astype(F32)
        misfit[NW * m + 1] = value
        kept[NW * m + 1] = value
        even = NW * lax.rem(m + 1, G)
        image = jnp.where(m == G - 1, before[...], im[1])
        value = inc[even] - image.astype(F32)
        misfit[even] = value
        kept[even] = value


def normal_kernel(kept, p0, p1, p2, p3, normal):
    y = member()
    for k, part in enumerate((p0, p1, p2, p3)):
        m = origin(y, k)
        for w in range(NW):
            normal[NW * m + w] = kept[NW * m + w] - part[w].astype(F32)


VMEM_LIMIT = 16 * 1024 * 1024
SMEM = pl.BlockSpec(memory_space=pltpu.SMEM)
VMEM = pl.BlockSpec(memory_space=pltpu.VMEM)


def sds(shape, dtype=BF):
    return jax.ShapeDtypeStruct(shape, dtype)


def call(kernel, ins, outs, scratch=(), smem=0):
    return pl.pallas_call(
        kernel,
        out_shape=outs,
        in_specs=[SMEM] * smem + [VMEM] * (len(ins) - smem),
        out_specs=[VMEM] * len(outs),
        scratch_shapes=list(scratch),
        compiler_params=pltpu.CompilerParams(vmem_limit_bytes=VMEM_LIMIT),
    )(*ins)


def group_pairs(k):
    return [(b, b // G * G + (b + k) % G) for b in range(PARTS)]


def side_pairs(d):
    return [(b, (b + G * d) % PARTS) for b in range(PARTS)]


def next_increment_pairs(k):
    pairs = []
    for t in range(TM):
        for b in range(PARTS):
            m = (b + k) % G
            if k == 0 and m != G - 1:
                continue
            to = (t - 1) % TM if m == G - 1 else t
            pairs.append((t * PARTS + b, to * PARTS + b // G * G + m))
    return pairs


def to_members(sends):
    return [lax.ppermute(sends[k], "mesh", group_pairs(k)) for k in range(1, G)]


def swap_sides(send_left, send_right):
    left = lax.ppermute(send_right, "mesh", side_pairs(1))
    right = lax.ppermute(send_left, "mesh", side_pairs(-1))
    return left, right


def local(states, increment, window_slots, edge_weights, inner_weight, inner_bias, outer_weight):
    bias = inner_bias

    item = sds((NW, 2, B, D))
    half = sds((NW, B, D))
    pair_bf = sds((NW, 2 * B, D))
    pair = sds((NW, 2 * B, D), F32)
    hidden = sds((NW, 2 * B, HID))
    mats = sds((G, B, 3 * B))
    hat = pltpu.VMEM((2 * B, 4 * B), BF)

    sends = call(pack_kernel, (states, increment), [item] * (G - 1))
    got = [None, *to_members([None, *sends])]
    got[0], cross, *ext = call(
        fold_kernel, (window_slots, states, increment, edge_weights),
        [item, sds((B, D))] + [sds((B, 6 * B + D))] * G, smem=1,
    )
    cross = lax.ppermute(cross, ("tm", "mesh"), next_increment_pairs(0))
    ext = [ext[0]] + [lax.ppermute(ext[k], ("tm", "mesh"), next_increment_pairs(k)) for k in range(1, G)]

    lo, hi = call(edge_kernel, got, [item, item])
    left, right = swap_sides(lo, hi)
    field, amat0, tmat0, base_in, tan_in, slope_in = call(
        inner0_kernel, (*got, *ext, inner_weight, bias, outer_weight),
        [sds((NW, G * B, 2 * D)), mats, mats, pair_bf, pair, hidden], (hat,)
    )
    lo, hi, tan_edge, slope_edge = call(
        edge0_kernel, (field, amat0, left, right, inner_weight, bias, outer_weight),
        [item, item, pair, hidden]
    )

    left, right = swap_sides(lo, hi)
    slope1 = pltpu.VMEM((2 * B, HID), BF)
    amat1, tmat1, next_edge, image_in, inner = call(
        inner1_kernel,
        (base_in, tan_in, lo, hi, field, ext[0], cross, *ext[1:], inner_weight, bias, outer_weight),
        [mats, mats, sds((2 * B, D)), pair_bf, pair],
        (hat, slope1, pltpu.VMEM((G, B, D), BF))
    )
    *images, edge, send_left, send_right = call(
        edge1_kernel,
        (lo, hi, tan_edge, base_in, tan_in, left, right, field, next_edge, amat1, tmat1, image_in,
         inner_weight, bias, outer_weight),
        [half] * G + [pair, half, half],
        (slope1, pltpu.VMEM((G, NW, B, D), BF))
    )

    left, right = swap_sides(send_left, send_right)
    images = [images[0], *to_members(images)]
    cur_edge, inner = call(
        inner2_kernel, (inner, edge, tmat1, slope_in, inner_weight, outer_weight),
        [pair, pair], (hat,)
    )
    edge, send_left, send_right = call(
        edge2_kernel, (cur_edge, left, right, tmat0, slope_edge, inner_weight, outer_weight),
        [pair, half, half]
    )

    left, right = swap_sides(send_left, send_right)
    cur_edge, cur_inner, last = call(
        inner3_kernel, (inner, edge, tmat0, *images), [pair, pair_bf, sds((B, D))], (hat,),
    )
    before = lax.ppermute(last, "tm", [(t, t + 1) for t in range(TM - 1)])
    parts = call(
        finish_kernel, (cur_edge, cur_inner, left, right), [half] * G,
        (pltpu.VMEM((G, NW, B, D), BF),),
    )
    parts = [parts[0], *to_members(parts)]
    whole = sds(increment.shape, F32)
    misfit, kept = call(misfit_kernel, (increment, *images, before), [whole, whole])
    (normal,) = call(normal_kernel, (kept, *parts), [whole])
    return misfit, normal


def solution(mesh):
    placed = (
        P("tm", "mesh", None),
        P("tm", "mesh", None),
        P("mesh", None),
        P(None, "mesh", None, None, None),
        P(),
        P(),
        P(),
    )

    return jax.shard_map(
        local,
        mesh=mesh,
        in_specs=placed,
        out_specs=(P("tm", "mesh", None), P("tm", "mesh", None)),
        check_vma=False,
    )
```

```python
import functools

import jax
import jax.numpy as jnp
from jax import lax
from jax.experimental import pallas as pl
from jax.experimental.pallas import tpu as pltpu
from jax.sharding import PartitionSpec as P


BF = jnp.bfloat16
F32 = jnp.float32
G = 4
NW = 2
B = 128
D = 256
HID = 1024
HC = 256
TM = 4
PARTS = 64
HALF_ROOT = 0.7071067811865476
DENSITY_NORM = 0.3989422804014327


def dot(a, b, ca=1, cb=0):
    return lax.dot_general(a, b, (((ca,), (cb,)), ((), ())), preferred_element_type=F32)


def member():
    return lax.rem(lax.axis_index("mesh"), G)


def last_member():
    return jnp.logical_and(member() == G - 1, lax.axis_index("tm") == TM - 1)


def origin(y, k):
    return lax.rem(y + G - k, G)


def stack(*values):
    return jnp.concatenate(values, axis=0)


def pack_kernel(states, inc, *outs):
    y = member()
    for w in range(NW):
        for k in range(1, G):
            m = lax.rem(y + k, G)
            outs[w * (G - 1) + k - 1][0] = states[NW * m + w]
            outs[w * (G - 1) + k - 1][1] = inc[NW * m + w].astype(BF)


def fold_kernel(slots, states, inc, edges, own0, own1, a0, cross, *ext):
    y = member()
    for w, own in enumerate((own0, own1)):
        own[0] = states[NW * y + w]
        own[1] = inc[NW * y + w].astype(BF)
    for layer in range(2):
        for slot in range(3):
            total = jnp.zeros((B, B), F32)
            for f in range(4):
                total += jnp.where(slots[0, f] == slot, edges[layer, 0, f].astype(F32), 0.0)
            cols = slice(slot * B, (slot + 1) * B)
            if layer == 0:
                a0[:, cols] = total.astype(BF)
            else:
                for k in range(G):
                    ext[k][:, cols] = total.astype(BF)
    for k in range(G):
        m = lax.rem(y + k + 1, G)
        value = inc[NW * m].astype(BF)
        ext[k][:, 3 * B :] = value
        if k == 0:
            cross[...] = value


def edge_kernel(r0, r1, r2, r3, send_left, send_right):
    y = member()
    for k, r in enumerate((r0, r1, r2, r3)):
        block = origin(y, k)

        @pl.when(block == 0)
        def _():
            send_left[...] = r[...]

        @pl.when(block == G - 1)
        def _():
            send_right[...] = r[...]


def sort_edges(y, mats, amat, tmat):
    for k, a in enumerate(mats):
        amat[origin(y, k)] = a[:, : 3 * B]
    for c in range(G):
        for slot in range(3):
            t = jnp.transpose(amat[c, :, slot * B : (slot + 1) * B].astype(F32)).astype(BF)
            to = c + slot - 1
            if 0 <= to < G:
                place = 2 - slot
            else:
                to, place = c, slot
            tmat[to, :, place * B : (place + 1) * B] = t


def pair_matrix(mats, hat):
    hat[0:B, 3 * B :] = jnp.zeros((B, B), BF)
    hat[B:, 0:B] = jnp.zeros((B, B), BF)
    hat[0:B, 0 : 3 * B] = mats[1]
    hat[B:, B:] = mats[2]


def forward_rows(base_sum, tan_sum, layer, win, bias, wout, slope, with_base):
    both = stack(base_sum.astype(BF), tan_sum.astype(BF))
    half = base_sum.shape[0]
    for h in range(HID // HC):
        cols = slice(h * HC, (h + 1) * HC)
        z = dot(both, win[layer, :, cols])
        act = z[:half] + bias[layer : layer + 1, cols]
        phi = 0.5 * (1.0 + lax.erf(act * HALF_ROOT))
        slp = phi + act * jnp.exp(-0.5 * act * act) * DENSITY_NORM
        slope[:, cols] = slp.astype(BF)
        lifted = (slp * z[half:]).astype(BF)
        tan_sum = tan_sum + dot(lifted, wout[layer, cols, :])
        if with_base:
            base_sum = base_sum + dot((act * phi).astype(BF), wout[layer, cols, :])
    return base_sum, tan_sum


def adjoint_rows(current, layer, win, wout, slope):
    narrow = current.astype(BF)
    for h in range(HID // HC):
        cols = slice(h * HC, (h + 1) * HC)
        up = dot(narrow, wout[layer, cols, :], 1, 1)
        pulled = (slope[:, cols].astype(F32) * up).astype(BF)
        current = current + dot(pulled, win[layer, :, cols], 1, 1)
    return current


def inner0_kernel(
    r00, r01, r02, r03, r10, r11, r12, r13, a0, a1, a2, a3, win, bias, wout,
    field, amat, tmat, base_out, tan_out, slope, hat,
):
    y = member()
    sort_edges(y, (a0, a1, a2, a3), amat, tmat)
    pair_matrix(amat, hat)
    for w, got in enumerate(((r00, r01, r02, r03), (r10, r11, r12, r13))):
        for k, r in enumerate(got):
            rows = pl.ds(pl.multiple_of(origin(y, k) * B, B), B)
            field[w, rows, 0:D] = r[0]
            field[w, rows, D:] = r[1]
    for w in range(NW):
        agg = dot(hat[...], field[w])
        base_sum = field[w, B : 3 * B, 0:D].astype(F32) + agg[:, 0:D]
        tan_sum = field[w, B : 3 * B, D:].astype(F32) + agg[:, D:]
        base, tan = forward_rows(base_sum, tan_sum, 0, win, bias, wout, slope.at[w], True)
        base_out[w] = base.astype(BF)
        tan_out[w] = tan


def edge0_kernel(
    w, field, amat, left, right, win, bias, wout,
    send_left, send_right, tan_out, slope,
):
    lo = stack(jnp.concatenate([left[0], left[1]], axis=1), field[w, 0 : 2 * B])
    hi = stack(field[w, 2 * B :], jnp.concatenate([right[0], right[1]], axis=1))
    agg = stack(dot(amat[0], lo), dot(amat[G - 1], hi))
    own = stack(field[w, 0:B], field[w, 3 * B :]).astype(F32)
    base, tan = forward_rows(
        own[:, 0:D] + agg[:, 0:D], own[:, D:] + agg[:, D:], 0, win, bias, wout, slope, True
    )
    tan_out[...] = tan
    base, tan = base.astype(BF), tan.astype(BF)
    send_left[0] = base[0:B]
    send_left[1] = tan[0:B]
    send_right[0] = base[B:]
    send_right[1] = tan[B:]


def inner1_kernel(
    base_in, tan_in, lo0, lo1, hi0, hi1, field, e0, e0r, e1, e2, e3, win, bias, wout,
    amat, tmat, next_out, image, returned, hat, slope, nxt,
):
    y = member()
    sort_edges(y, (e0, e1, e2, e3), amat, tmat)
    pair_matrix(amat, hat)
    for k, e in enumerate((e0, e1, e2, e3)):
        value = e[:, 3 * B :]
        if k == 0:
            value = jnp.where(y == G - 1, e0r[...], value)
        nxt[origin(y, k)] = value
    next_out[0:B] = nxt[0]
    next_out[B:] = nxt[G - 1]
    for w in range(NW):
        lo, hi = (lo0, lo1)[w], (hi0, hi1)[w]
        base = stack(lo[0], base_in[w], hi[0])
        tan = stack(lo[1], tan_in[w].astype(BF), hi[1])
        base_sum = base_in[w].astype(F32) + dot(hat[...], base)
        tan_sum = tan_in[w] + dot(hat[...], tan)
        _, out = forward_rows(base_sum, tan_sum, 1, win, bias, wout, slope, False)
        image[w] = out.astype(BF)
        if w == 0:
            following = field[1, B : 3 * B, D:].astype(F32)
            current = following - out
        else:
            following = stack(nxt[1], nxt[2]).astype(F32)
            current = jnp.where(last_member(), 0.0, following - out)
        returned[w] = adjoint_rows(current, 1, win, wout, slope)


def edge1_kernel(
    lo0, lo1, hi0, hi1, tan0, tan1, left0, left1, right0, right1, base_in, tan_in, field, next_edge, amat, tmat, image_in, win, bias, wout,
    im0, im1, im2, im3, returned, send_left, send_right, slope, image,
):
    y = member()
    for w in range(NW):
        lo, hi, tan_edge = (lo0, lo1)[w], (hi0, hi1)[w], (tan0, tan1)[w]
        left, right = (left0, left1)[w], (right0, right1)[w]
        tan_mid = tan_in[w].astype(BF)
        agg = []
        for f, mid in ((0, base_in[w]), (1, tan_mid)):
            agg.append(stack(
                dot(amat[0], stack(left[f], lo[f], mid[0:B])),
                dot(amat[G - 1], stack(mid[B:], hi[f], right[f])),
            ))
        base_sum = stack(lo[0], hi[0]).astype(F32) + agg[0]
        _, out = forward_rows(base_sum, tan_edge[...] + agg[1], 1, win, bias, wout, slope, False)
        image[0, w] = out[0:B].astype(BF)
        image[1, w] = image_in[w, 0:B]
        image[2, w] = image_in[w, B:]
        image[3, w] = out[B:].astype(BF)
        if w == 0:
            following = stack(field[1, 0:B, D:], field[1, 3 * B :, D:]).astype(F32)
            current = following - out
        else:
            current = jnp.where(last_member(), 0.0, next_edge[...].astype(F32) - out)
        back = adjoint_rows(current, 1, win, wout, slope)
        returned[w] = back
        send_left[w] = dot(tmat[0, :, 0:B], back[0:B].astype(BF)).astype(BF)
        send_right[w] = dot(tmat[G - 1, :, 2 * B :], back[B:].astype(BF)).astype(BF)
    for k, im in enumerate((im0, im1, im2, im3)):
        im[...] = image[lax.rem(y + k, G)]


def spread_edge(tmat, edge, narrow):
    return edge + stack(
        dot(tmat[0, :, B:], narrow[0 : 2 * B]), dot(tmat[G - 1, :, 0 : 2 * B], narrow[2 * B :])
    )


def inner2_kernel(inner, edge, tmat, slope, win, wout, cur_edge, returned, hat):
    pair_matrix(tmat, hat)
    for w in range(NW):
        narrow = stack(edge[w, 0:B], inner[w], edge[w, B:]).astype(BF)
        cur_edge[w] = spread_edge(tmat, edge[w], narrow)
        current = inner[w] + dot(hat[...], narrow)
        returned[w] = adjoint_rows(current, 0, win, wout, slope.at[w])


def edge2_kernel(cur_edge, left, right, tmat, slope0, slope1, win, wout, returned, send_left, send_right):
    for w in range(NW):
        current = cur_edge[w] + stack(left[w], right[w]).astype(F32)
        back = adjoint_rows(current, 0, win, wout, (slope0, slope1)[w])
        returned[w] = back
        send_left[w] = dot(tmat[0, :, 0:B], back[0:B].astype(BF)).astype(BF)
        send_right[w] = dot(tmat[G - 1, :, 2 * B :], back[B:].astype(BF)).astype(BF)


def inner3_kernel(inner, edge, tmat, i0, i1, i2, i3, cur_edge, cur_inner, last, hat):
    y = member()
    for k, im in enumerate((i0, i1, i2, i3)):

        @pl.when(origin(y, k) == G - 1)
        def _():
            last[...] = im[NW - 1]

    pair_matrix(tmat, hat)
    for w in range(NW):
        narrow = stack(edge[w, 0:B], inner[w], edge[w, B:]).astype(BF)
        cur_edge[w] = spread_edge(tmat, edge[w], narrow)
        cur_inner[w] = (inner[w] + dot(hat[...], narrow)).astype(BF)


def finish_kernel(cur_edge, cur_inner, left, right, o0, o1, o2, o3, all_blocks):
    y = member()
    for w in range(NW):
        all_blocks[0, w] = (cur_edge[w, 0:B] + left[w].astype(F32)).astype(BF)
        all_blocks[1, w] = cur_inner[w, 0:B]
        all_blocks[2, w] = cur_inner[w, B:]
        all_blocks[3, w] = (cur_edge[w, B:] + right[w].astype(F32)).astype(BF)
    for k, out in enumerate((o0, o1, o2, o3)):
        out[...] = all_blocks[lax.rem(y + k, G)]


def misfit_kernel(inc, i0, i1, i2, i3, before, misfit, kept):
    y = member()
    for k, im in enumerate((i0, i1, i2, i3)):
        m = origin(y, k)
        value = inc[NW * m + 1] - im[0].astype(F32)
        misfit[NW * m + 1] = value
        kept[NW * m + 1] = value
        even = NW * lax.rem(m + 1, G)
        image = jnp.where(m == G - 1, before[...], im[1])
        value = inc[even] - image.astype(F32)
        misfit[even] = value
        kept[even] = value


def normal_kernel(kept, p0, p1, p2, p3, normal):
    y = member()
    for k, part in enumerate((p0, p1, p2, p3)):
        m = origin(y, k)
        for w in range(NW):
            normal[NW * m + w] = kept[NW * m + w] - part[w].astype(F32)


VMEM_LIMIT = 16 * 1024 * 1024
SMEM = pl.BlockSpec(memory_space=pltpu.SMEM)
VMEM = pl.BlockSpec(memory_space=pltpu.VMEM)


def sds(shape, dtype=BF):
    return jax.ShapeDtypeStruct(shape, dtype)


def call(kernel, ins, outs, scratch=(), smem=0):
    return pl.pallas_call(
        kernel,
        out_shape=outs,
        in_specs=[SMEM] * smem + [VMEM] * (len(ins) - smem),
        out_specs=[VMEM] * len(outs),
        scratch_shapes=list(scratch),
        compiler_params=pltpu.CompilerParams(vmem_limit_bytes=VMEM_LIMIT),
    )(*ins)


def group_pairs(k):
    return [(b, b // G * G + (b + k) % G) for b in range(PARTS)]


def side_pairs(d):
    return [(b, (b + G * d) % PARTS) for b in range(PARTS)]


def next_increment_pairs(k):
    pairs = []
    for t in range(TM):
        for b in range(PARTS):
            m = (b + k) % G
            if k == 0 and m != G - 1:
                continue
            to = (t - 1) % TM if m == G - 1 else t
            pairs.append((t * PARTS + b, to * PARTS + b // G * G + m))
    return pairs


def to_members(sends):
    return [lax.ppermute(sends[k], "mesh", group_pairs(k)) for k in range(1, G)]


def swap_sides(send_left, send_right):
    left = lax.ppermute(send_right, "mesh", side_pairs(1))
    right = lax.ppermute(send_left, "mesh", side_pairs(-1))
    return left, right


def local(states, increment, window_slots, edge_weights, inner_weight, inner_bias, outer_weight):

    item = sds((2, B, D))
    half = sds((NW, B, D))
    pair_bf = sds((NW, 2 * B, D))
    pair = sds((NW, 2 * B, D), F32)
    hidden = sds((NW, 2 * B, HID))
    mats = sds((G, B, 3 * B))
    hat = pltpu.VMEM((2 * B, 4 * B), BF)
    weights = (inner_weight, inner_bias, outer_weight)
    both = ("tm", "mesh")

    sends = call(pack_kernel, (states, increment), [item] * (NW * (G - 1)))
    got = [to_members([None, *sends[w * (G - 1) : (w + 1) * (G - 1)]]) for w in range(NW)]
    *own, a0, cross, ext, ext1, ext2, ext3 = call(
        fold_kernel, (window_slots, states, increment, edge_weights),
        [item] * NW + [sds((B, 3 * B)), sds((B, D))] + [sds((B, 3 * B + D))] * G, smem=1,
    )
    a0 = [a0, *to_members([a0] * G)]
    cross = lax.ppermute(cross, both, next_increment_pairs(0))
    ext = [ext, cross] + [
        lax.ppermute(e, both, next_increment_pairs(k + 1)) for k, e in enumerate((ext1, ext2, ext3))
    ]

    got = [[own[w], *got[w]] for w in range(NW)]
    halo = []
    for w in range(NW):
        lo, hi = call(edge_kernel, got[w], [item, item])
        halo.append(swap_sides(lo, hi))
    field, amat0, tmat0, base_in, tan_in, slope_in = call(
        inner0_kernel, (*got[0], *got[1], *a0, *weights),
        [sds((NW, G * B, 2 * D)), mats, mats, pair_bf, pair, hidden], (hat,),
    )
    lo, hi, tan_edge, slope_edge, left, right = [], [], [], [], [], []
    for w in range(NW):
        out = call(
            functools.partial(edge0_kernel, w), (field, amat0, *halo[w], *weights),
            [item, item, sds((2 * B, D), F32), sds((2 * B, HID))],
        )
        for values, value in zip((lo, hi, tan_edge, slope_edge), out):
            values.append(value)
        for values, value in zip((left, right), swap_sides(out[0], out[1])):
            values.append(value)

    slope1 = pltpu.VMEM((2 * B, HID), BF)
    amat1, tmat1, next_edge, image_in, inner = call(
        inner1_kernel, (base_in, tan_in, *lo, *hi, field, *ext, *weights),
        [mats, mats, sds((2 * B, D)), pair_bf, pair], (hat, slope1, pltpu.VMEM((G, B, D), BF)),
    )
    *images, edge, send_left, send_right = call(
        edge1_kernel,
        (*lo, *hi, *tan_edge, *left, *right, base_in, tan_in, field, next_edge, amat1, tmat1, image_in, *weights),
        [half] * G + [pair, half, half], (slope1, pltpu.VMEM((G, NW, B, D), BF)),
    )

    left, right = swap_sides(send_left, send_right)
    images = [images[0], *to_members(images)]
    cur_edge, inner = call(
        inner2_kernel, (inner, edge, tmat1, slope_in, inner_weight, outer_weight),
        [pair, pair], (hat,)
    )
    edge, send_left, send_right = call(
        edge2_kernel, (cur_edge, left, right, tmat0, *slope_edge, inner_weight, outer_weight),
        [pair, half, half]
    )

    left, right = swap_sides(send_left, send_right)
    cur_edge, cur_inner, last = call(
        inner3_kernel, (inner, edge, tmat0, *images), [pair, pair_bf, sds((B, D))], (hat,),
    )
    before = lax.ppermute(last, "tm", [(t, t + 1) for t in range(TM - 1)])
    parts = call(
        finish_kernel, (cur_edge, cur_inner, left, right), [half] * G,
        (pltpu.VMEM((G, NW, B, D), BF),),
    )
    parts = [parts[0], *to_members(parts)]
    whole = sds(increment.shape, F32)
    misfit, kept = call(misfit_kernel, (increment, *images, before), [whole, whole])
    (normal,) = call(normal_kernel, (kept, *parts), [whole])
    return misfit, normal


def solution(mesh):
    placed = (
        P("tm", "mesh", None),
        P("tm", "mesh", None),
        P("mesh", None),
        P(None, "mesh", None, None, None),
        P(),
        P(),
        P(),
    )

    return jax.shard_map(
        local,
        mesh=mesh,
        in_specs=placed,
        out_specs=(P("tm", "mesh", None), P("tm", "mesh", None)),
        check_vma=False,
    )
```

```python
import functools

import jax
import jax.numpy as jnp
from jax import lax
from jax.experimental import pallas as pl
from jax.experimental.pallas import tpu as pltpu
from jax.sharding import PartitionSpec as P


BF = jnp.bfloat16
F32 = jnp.float32
G = 4
NW = 2
B = 128
D = 256
HID = 1024
HC = 256
TM = 4
PARTS = 64
HALF_ROOT = 0.7071067811865476
DENSITY_NORM = 0.3989422804014327


def dot(a, b, ca=1, cb=0):
    return lax.dot_general(a, b, (((ca,), (cb,)), ((), ())), preferred_element_type=F32)


def member():
    return lax.rem(lax.axis_index("mesh"), G)


def last_member():
    return jnp.logical_and(member() == G - 1, lax.axis_index("tm") == TM - 1)


def origin(y, k):
    return lax.rem(y + G - k, G)


def stack(*values):
    return jnp.concatenate(values, axis=0)


def pack_kernel(states, inc, *outs):
    y = member()
    for w in range(NW):
        for k in range(1, G):
            m = lax.rem(y + k, G)
            outs[w * (G - 1) + k - 1][0] = states[NW * m + w]
            outs[w * (G - 1) + k - 1][1] = inc[NW * m + w].astype(BF)


def fold_kernel(slots, states, inc, edges, own0, own1, folded):
    y = member()
    for w, own in enumerate((own0, own1)):
        own[0] = states[NW * y + w]
        own[1] = inc[NW * y + w].astype(BF)
    for layer in range(2):
        for slot in range(3):
            total = jnp.zeros((B, B), F32)
            for f in range(4):
                total += jnp.where(slots[0, f] == slot, edges[layer, 0, f].astype(F32), 0.0)
            first = (3 * layer + slot) * B
            folded[:, first : first + B] = total.astype(BF)


def edge_kernel(r0, r1, r2, r3, send_left, send_right, inc=None):
    y = member()
    for k, r in enumerate((r0, r1, r2, r3)):
        block = origin(y, k)
        if inc is not None:
            inc[block] = r[1]

        @pl.when(block == 0)
        def _():
            send_left[...] = r[...]

        @pl.when(block == G - 1)
        def _():
            send_right[...] = r[...]


def sort_edges(y, mats, layer, amat, tmat):
    for k, a in enumerate(mats):
        amat[origin(y, k)] = a[:, 3 * layer * B : 3 * (layer + 1) * B]
    for c in range(G):
        for slot in range(3):
            t = jnp.transpose(amat[c, :, slot * B : (slot + 1) * B].astype(F32)).astype(BF)
            to = c + slot - 1
            if 0 <= to < G:
                place = 2 - slot
            else:
                to, place = c, slot
            tmat[to, :, place * B : (place + 1) * B] = t


def pair_matrix(mats, hat):
    hat[0:B, 3 * B :] = jnp.zeros((B, B), BF)
    hat[B:, 0:B] = jnp.zeros((B, B), BF)
    hat[0:B, 0 : 3 * B] = mats[1]
    hat[B:, B:] = mats[2]


def forward_rows(base_sum, tan_sum, layer, win, bias, wout, slope, with_base):
    both = stack(base_sum.astype(BF), tan_sum.astype(BF))
    half = base_sum.shape[0]
    for h in range(HID // HC):
        cols = slice(h * HC, (h + 1) * HC)
        z = dot(both, win[layer, :, cols])
        act = z[:half] + bias[layer : layer + 1, cols]
        phi = 0.5 * (1.0 + lax.erf(act * HALF_ROOT))
        slp = phi + act * jnp.exp(-0.5 * act * act) * DENSITY_NORM
        slope[:, cols] = slp.astype(BF)
        lifted = (slp * z[half:]).astype(BF)
        tan_sum = tan_sum + dot(lifted, wout[layer, cols, :])
        if with_base:
            base_sum = base_sum + dot((act * phi).astype(BF), wout[layer, cols, :])
    return base_sum, tan_sum


def adjoint_rows(current, layer, win, wout, slope):
    narrow = current.astype(BF)
    for h in range(HID // HC):
        cols = slice(h * HC, (h + 1) * HC)
        up = dot(narrow, wout[layer, cols, :], 1, 1)
        pulled = (slope[:, cols].astype(F32) * up).astype(BF)
        current = current + dot(pulled, win[layer, :, cols], 1, 1)
    return current


def inner0_kernel(
    r00, r01, r02, r03, r10, r11, r12, r13, a0, a1, a2, a3, win, bias, wout,
    field, amat, tmat, base_out, tan_out, slope, hat,
):
    y = member()
    sort_edges(y, (a0, a1, a2, a3), 0, amat, tmat)
    pair_matrix(amat, hat)
    for w, got in enumerate(((r00, r01, r02, r03), (r10, r11, r12, r13))):
        for k, r in enumerate(got):
            rows = pl.ds(pl.multiple_of(origin(y, k) * B, B), B)
            field[w, rows, 0:D] = r[0]
            field[w, rows, D:] = r[1]
    for w in range(NW):
        agg = dot(hat[...], field[w])
        base_sum = field[w, B : 3 * B, 0:D].astype(F32) + agg[:, 0:D]
        tan_sum = field[w, B : 3 * B, D:].astype(F32) + agg[:, D:]
        base, tan = forward_rows(base_sum, tan_sum, 0, win, bias, wout, slope.at[w], True)
        base_out[w] = base.astype(BF)
        tan_out[w] = tan


def edge0_kernel(
    w, field, amat, left, right, win, bias, wout,
    send_left, send_right, tan_out, slope,
):
    lo = stack(jnp.concatenate([left[0], left[1]], axis=1), field[w, 0 : 2 * B])
    hi = stack(field[w, 2 * B :], jnp.concatenate([right[0], right[1]], axis=1))
    agg = stack(dot(amat[0], lo), dot(amat[G - 1], hi))
    own = stack(field[w, 0:B], field[w, 3 * B :]).astype(F32)
    base, tan = forward_rows(
        own[:, 0:D] + agg[:, 0:D], own[:, D:] + agg[:, D:], 0, win, bias, wout, slope, True
    )
    tan_out[...] = tan
    base, tan = base.astype(BF), tan.astype(BF)
    send_left[0] = base[0:B]
    send_left[1] = tan[0:B]
    send_right[0] = base[B:]
    send_right[1] = tan[B:]


def inner1_kernel(
    base_in, tan_in, lo0, lo1, hi0, hi1, field, a0, a1, a2, a3, nxt, win, bias, wout,
    amat, tmat, image, returned, hat, slope,
):
    y = member()
    sort_edges(y, (a0, a1, a2, a3), 1, amat, tmat)
    pair_matrix(amat, hat)
    for w in range(NW):
        lo, hi = (lo0, lo1)[w], (hi0, hi1)[w]
        base = stack(lo[0], base_in[w], hi[0])
        tan = stack(lo[1], tan_in[w].astype(BF), hi[1])
        base_sum = base_in[w].astype(F32) + dot(hat[...], base)
        tan_sum = tan_in[w] + dot(hat[...], tan)
        _, out = forward_rows(base_sum, tan_sum, 1, win, bias, wout, slope, False)
        image[w] = out.astype(BF)
        if w == 0:
            following = field[1, B : 3 * B, D:].astype(F32)
            current = following - out
        else:
            following = stack(nxt[1], nxt[2]).astype(F32)
            current = jnp.where(last_member(), 0.0, following - out)
        returned[w] = adjoint_rows(current, 1, win, wout, slope)


def edge1_kernel(
    lo0, lo1, hi0, hi1, tan0, tan1, left0, left1, right0, right1, base_in, tan_in, field, nxt, amat, tmat, image_in, win, bias, wout,
    im0, im1, im2, im3, returned, send_left, send_right, slope, image,
):
    y = member()
    for w in range(NW):
        lo, hi, tan_edge = (lo0, lo1)[w], (hi0, hi1)[w], (tan0, tan1)[w]
        left, right = (left0, left1)[w], (right0, right1)[w]
        tan_mid = tan_in[w].astype(BF)
        agg = []
        for f, mid in ((0, base_in[w]), (1, tan_mid)):
            agg.append(stack(
                dot(amat[0], stack(left[f], lo[f], mid[0:B])),
                dot(amat[G - 1], stack(mid[B:], hi[f], right[f])),
            ))
        base_sum = stack(lo[0], hi[0]).astype(F32) + agg[0]
        _, out = forward_rows(base_sum, tan_edge[...] + agg[1], 1, win, bias, wout, slope, False)
        image[0, w] = out[0:B].astype(BF)
        image[1, w] = image_in[w, 0:B]
        image[2, w] = image_in[w, B:]
        image[3, w] = out[B:].astype(BF)
        if w == 0:
            following = stack(field[1, 0:B, D:], field[1, 3 * B :, D:]).astype(F32)
            current = following - out
        else:
            current = jnp.where(last_member(), 0.0, stack(nxt[0], nxt[G - 1]).astype(F32) - out)
        back = adjoint_rows(current, 1, win, wout, slope)
        returned[w] = back
        send_left[w] = dot(tmat[0, :, 0:B], back[0:B].astype(BF)).astype(BF)
        send_right[w] = dot(tmat[G - 1, :, 2 * B :], back[B:].astype(BF)).astype(BF)
    for k, im in enumerate((im0, im1, im2, im3)):
        im[...] = image[lax.rem(y + k, G)]


def spread_edge(tmat, edge, narrow):
    return edge + stack(
        dot(tmat[0, :, B:], narrow[0 : 2 * B]), dot(tmat[G - 1, :, 0 : 2 * B], narrow[2 * B :])
    )


def inner2_kernel(inner, edge, tmat, slope, win, wout, cur_edge, returned, hat):
    pair_matrix(tmat, hat)
    for w in range(NW):
        narrow = stack(edge[w, 0:B], inner[w], edge[w, B:]).astype(BF)
        cur_edge[w] = spread_edge(tmat, edge[w], narrow)
        current = inner[w] + dot(hat[...], narrow)
        returned[w] = adjoint_rows(current, 0, win, wout, slope.at[w])


def edge2_kernel(cur_edge, left, right, tmat, slope0, slope1, win, wout, returned, send_left, send_right):
    for w in range(NW):
        current = cur_edge[w] + stack(left[w], right[w]).astype(F32)
        back = adjoint_rows(current, 0, win, wout, (slope0, slope1)[w])
        returned[w] = back
        send_left[w] = dot(tmat[0, :, 0:B], back[0:B].astype(BF)).astype(BF)
        send_right[w] = dot(tmat[G - 1, :, 2 * B :], back[B:].astype(BF)).astype(BF)


def inner3_kernel(inner, edge, tmat, i0, i1, i2, i3, cur_edge, cur_inner, last, hat):
    y = member()
    for k, im in enumerate((i0, i1, i2, i3)):

        @pl.when(origin(y, k) == G - 1)
        def _():
            last[...] = im[NW - 1]

    pair_matrix(tmat, hat)
    for w in range(NW):
        narrow = stack(edge[w, 0:B], inner[w], edge[w, B:]).astype(BF)
        cur_edge[w] = spread_edge(tmat, edge[w], narrow)
        cur_inner[w] = (inner[w] + dot(hat[...], narrow)).astype(BF)


def finish_kernel(cur_edge, cur_inner, left, right, o0, o1, o2, o3, all_blocks):
    y = member()
    for w in range(NW):
        all_blocks[0, w] = (cur_edge[w, 0:B] + left[w].astype(F32)).astype(BF)
        all_blocks[1, w] = cur_inner[w, 0:B]
        all_blocks[2, w] = cur_inner[w, B:]
        all_blocks[3, w] = (cur_edge[w, B:] + right[w].astype(F32)).astype(BF)
    for k, out in enumerate((o0, o1, o2, o3)):
        out[...] = all_blocks[lax.rem(y + k, G)]


def misfit_kernel(inc, i0, i1, i2, i3, before, misfit, kept):
    y = member()
    for k, im in enumerate((i0, i1, i2, i3)):
        m = origin(y, k)
        value = inc[NW * m + 1] - im[0].astype(F32)
        misfit[NW * m + 1] = value
        kept[NW * m + 1] = value
        even = NW * lax.rem(m + 1, G)
        image = jnp.where(m == G - 1, before[...], im[1])
        value = inc[even] - image.astype(F32)
        misfit[even] = value
        kept[even] = value


def normal_kernel(kept, p0, p1, p2, p3, normal):
    y = member()
    for k, part in enumerate((p0, p1, p2, p3)):
        m = origin(y, k)
        for w in range(NW):
            normal[NW * m + w] = kept[NW * m + w] - part[w].astype(F32)


VMEM_LIMIT = 16 * 1024 * 1024
SMEM = pl.BlockSpec(memory_space=pltpu.SMEM)
VMEM = pl.BlockSpec(memory_space=pltpu.VMEM)


def sds(shape, dtype=BF):
    return jax.ShapeDtypeStruct(shape, dtype)


def call(kernel, ins, outs, scratch=(), smem=0):
    return pl.pallas_call(
        kernel,
        out_shape=outs,
        in_specs=[SMEM] * smem + [VMEM] * (len(ins) - smem),
        out_specs=[VMEM] * len(outs),
        scratch_shapes=list(scratch),
        compiler_params=pltpu.CompilerParams(vmem_limit_bytes=VMEM_LIMIT),
    )(*ins)


def group_pairs(k):
    return [(b, b // G * G + (b + k) % G) for b in range(PARTS)]


def side_pairs(d):
    return [(b, (b + G * d) % PARTS) for b in range(PARTS)]


def next_increment_pairs():
    pairs = []
    for t in range(TM):
        for b in range(PARTS):
            to = (t - 1) % TM if b % G == 0 else t
            pairs.append((t * PARTS + b, to * PARTS + b // G * G + (b - 1) % G))
    return pairs


def to_members(sends):
    return [lax.ppermute(sends[k], "mesh", group_pairs(k)) for k in range(1, G)]


def swap_sides(send_left, send_right):
    left = lax.ppermute(send_right, "mesh", side_pairs(1))
    right = lax.ppermute(send_left, "mesh", side_pairs(-1))
    return left, right


def local(states, increment, window_slots, edge_weights, inner_weight, inner_bias, outer_weight):

    item = sds((2, B, D))
    half = sds((NW, B, D))
    pair_bf = sds((NW, 2 * B, D))
    pair = sds((NW, 2 * B, D), F32)
    hidden = sds((NW, 2 * B, HID))
    mats = sds((G, B, 3 * B))
    hat = pltpu.VMEM((2 * B, 4 * B), BF)
    weights = (inner_weight, inner_bias, outer_weight)

    sends = call(pack_kernel, (states, increment), [item] * (NW * (G - 1)))
    got = [to_members([None, *sends[w * (G - 1) : (w + 1) * (G - 1)]]) for w in range(NW)]
    *own, folded = call(
        fold_kernel, (window_slots, states, increment, edge_weights),
        [item] * NW + [sds((B, 6 * B))], smem=1,
    )
    folded = [folded, *to_members([folded] * G)]

    got = [[own[w], *got[w]] for w in range(NW)]
    lo, hi, nxt = call(edge_kernel, got[0], [item, item, sds((G, B, D))])
    halo = [swap_sides(lo, hi)]
    lo, hi = call(edge_kernel, got[1], [item, item])
    halo.append(swap_sides(lo, hi))
    nxt = lax.ppermute(nxt, ("tm", "mesh"), next_increment_pairs())
    field, amat0, tmat0, base_in, tan_in, slope_in = call(
        inner0_kernel, (*got[0], *got[1], *folded, *weights),
        [sds((NW, G * B, 2 * D)), mats, mats, pair_bf, pair, hidden], (hat,),
    )
    lo, hi, tan_edge, slope_edge, left, right = [], [], [], [], [], []
    for w in range(NW):
        out = call(
            functools.partial(edge0_kernel, w), (field, amat0, *halo[w], *weights),
            [item, item, sds((2 * B, D), F32), sds((2 * B, HID))],
        )
        for values, value in zip((lo, hi, tan_edge, slope_edge), out):
            values.append(value)
        for values, value in zip((left, right), swap_sides(out[0], out[1])):
            values.append(value)

    slope1 = pltpu.VMEM((2 * B, HID), BF)
    amat1, tmat1, image_in, inner = call(
        inner1_kernel, (base_in, tan_in, *lo, *hi, field, *folded, nxt, *weights),
        [mats, mats, pair_bf, pair], (hat, slope1),
    )
    *images, edge, send_left, send_right = call(
        edge1_kernel,
        (*lo, *hi, *tan_edge, *left, *right, base_in, tan_in, field, nxt, amat1, tmat1, image_in, *weights),
        [half] * G + [pair, half, half], (slope1, pltpu.VMEM((G, NW, B, D), BF)),
    )

    left, right = swap_sides(send_left, send_right)
    images = [images[0], *to_members(images)]
    cur_edge, inner = call(
        inner2_kernel, (inner, edge, tmat1, slope_in, inner_weight, outer_weight),
        [pair, pair], (hat,)
    )
    edge, send_left, send_right = call(
        edge2_kernel, (cur_edge, left, right, tmat0, *slope_edge, inner_weight, outer_weight),
        [pair, half, half]
    )

    left, right = swap_sides(send_left, send_right)
    cur_edge, cur_inner, last = call(
        inner3_kernel, (inner, edge, tmat0, *images), [pair, pair_bf, sds((B, D))], (hat,),
    )
    before = lax.ppermute(last, "tm", [(t, t + 1) for t in range(TM - 1)])
    parts = call(
        finish_kernel, (cur_edge, cur_inner, left, right), [half] * G,
        (pltpu.VMEM((G, NW, B, D), BF),),
    )
    parts = [parts[0], *to_members(parts)]
    whole = sds(increment.shape, F32)
    misfit, kept = call(misfit_kernel, (increment, *images, before), [whole, whole])
    (normal,) = call(normal_kernel, (kept, *parts), [whole])
    return misfit, normal


def solution(mesh):
    placed = (
        P("tm", "mesh", None),
        P("tm", "mesh", None),
        P("mesh", None),
        P(None, "mesh", None, None, None),
        P(),
        P(),
        P(),
    )

    return jax.shard_map(
        local,
        mesh=mesh,
        in_specs=placed,
        out_specs=(P("tm", "mesh", None), P("tm", "mesh", None)),
        check_vma=False,
    )
```

```python
import functools

import jax
import jax.numpy as jnp
from jax import lax
from jax.experimental import pallas as pl
from jax.experimental.pallas import tpu as pltpu
from jax.sharding import PartitionSpec as P


BF = jnp.bfloat16
F32 = jnp.float32
G = 4
NW = 2
B = 128
D = 256
HID = 1024
HC = 256
TM = 4
PARTS = 64
HALF_ROOT = 0.7071067811865476
DENSITY_NORM = 0.3989422804014327


def dot(a, b, ca=1, cb=0):
    return lax.dot_general(a, b, (((ca,), (cb,)), ((), ())), preferred_element_type=F32)


def member():
    return lax.rem(lax.axis_index("mesh"), G)


def last_member():
    return jnp.logical_and(member() == G - 1, lax.axis_index("tm") == TM - 1)


def origin(y, k):
    return lax.rem(y + G - k, G)


def stack(*values):
    return jnp.concatenate(values, axis=0)


def pack_kernel(states, inc, *outs):
    y = member()
    for w in range(NW):
        for k in range(1, G):
            m = lax.rem(y + k, G)
            outs[w * (G - 1) + k - 1][0] = states[NW * m + w]
            outs[w * (G - 1) + k - 1][1] = inc[NW * m + w].astype(BF)


def fold_kernel(slots, states, inc, edges, own0, own1, folded):
    y = member()
    for w, own in enumerate((own0, own1)):
        own[0] = states[NW * y + w]
        own[1] = inc[NW * y + w].astype(BF)
    for layer in range(2):
        for slot in range(3):
            total = jnp.zeros((B, B), F32)
            for f in range(4):
                total += jnp.where(slots[0, f] == slot, edges[layer, 0, f].astype(F32), 0.0)
            first = (3 * layer + slot) * B
            folded[:, first : first + B] = total.astype(BF)


def edge_kernel(r0, r1, r2, r3, send_left, send_right, inc=None):
    y = member()
    for k, r in enumerate((r0, r1, r2, r3)):
        block = origin(y, k)
        if inc is not None:
            inc[block] = r[1]

        @pl.when(block == 0)
        def _():
            send_left[...] = r[...]

        @pl.when(block == G - 1)
        def _():
            send_right[...] = r[...]


def sort_edges(y, mats, layer, amat, tmat):
    for k, a in enumerate(mats):
        amat[origin(y, k)] = a[:, 3 * layer * B : 3 * (layer + 1) * B]
    for c in range(G):
        for slot in range(3):
            t = jnp.transpose(amat[c, :, slot * B : (slot + 1) * B].astype(F32)).astype(BF)
            to = c + slot - 1
            if 0 <= to < G:
                place = 2 - slot
            else:
                to, place = c, slot
            tmat[to, :, place * B : (place + 1) * B] = t


def pair_matrix(mats, hat):
    hat[0:B, 3 * B :] = jnp.zeros((B, B), BF)
    hat[B:, 0:B] = jnp.zeros((B, B), BF)
    hat[0:B, 0 : 3 * B] = mats[1]
    hat[B:, B:] = mats[2]


def forward_rows(base_sum, tan_sum, layer, win, bias, wout, slope, with_base):
    both = stack(base_sum.astype(BF), tan_sum.astype(BF))
    half = base_sum.shape[0]
    for h in range(HID // HC):
        cols = slice(h * HC, (h + 1) * HC)
        z = dot(both, win[layer, :, cols])
        act = z[:half] + bias[layer : layer + 1, cols]
        phi = 0.5 * (1.0 + lax.erf(act * HALF_ROOT))
        slp = phi + act * jnp.exp(-0.5 * act * act) * DENSITY_NORM
        slope[:, cols] = slp.astype(BF)
        lifted = (slp * z[half:]).astype(BF)
        tan_sum = tan_sum + dot(lifted, wout[layer, cols, :])
        if with_base:
            base_sum = base_sum + dot((act * phi).astype(BF), wout[layer, cols, :])
    return base_sum, tan_sum


def adjoint_rows(current, layer, win, wout, slope):
    narrow = current.astype(BF)
    for h in range(HID // HC):
        cols = slice(h * HC, (h + 1) * HC)
        up = dot(narrow, wout[layer, cols, :], 1, 1)
        pulled = (slope[:, cols].astype(F32) * up).astype(BF)
        current = current + dot(pulled, win[layer, :, cols], 1, 1)
    return current


def inner0_kernel(
    r00, r01, r02, r03, r10, r11, r12, r13, a0, a1, a2, a3, win, bias, wout,
    field, amat, tmat, base_out, tan_out, slope, hat,
):
    y = member()
    sort_edges(y, (a0, a1, a2, a3), 0, amat, tmat)
    pair_matrix(amat, hat)
    for w, got in enumerate(((r00, r01, r02, r03), (r10, r11, r12, r13))):
        for k, r in enumerate(got):
            rows = pl.ds(pl.multiple_of(origin(y, k) * B, B), B)
            field[w, rows, 0:D] = r[0]
            field[w, rows, D:] = r[1]
    for w in range(NW):
        agg = dot(hat[...], field[w])
        base_sum = field[w, B : 3 * B, 0:D].astype(F32) + agg[:, 0:D]
        tan_sum = field[w, B : 3 * B, D:].astype(F32) + agg[:, D:]
        base, tan = forward_rows(base_sum, tan_sum, 0, win, bias, wout, slope.at[w], True)
        base_out[w] = base.astype(BF)
        tan_out[w] = tan


def edge0_kernel(
    w, field, amat, left, right, win, bias, wout,
    send_left, send_right, tan_out, slope,
):
    lo = stack(jnp.concatenate([left[0], left[1]], axis=1), field[w, 0 : 2 * B])
    hi = stack(field[w, 2 * B :], jnp.concatenate([right[0], right[1]], axis=1))
    agg = stack(dot(amat[0], lo), dot(amat[G - 1], hi))
    own = stack(field[w, 0:B], field[w, 3 * B :]).astype(F32)
    base, tan = forward_rows(
        own[:, 0:D] + agg[:, 0:D], own[:, D:] + agg[:, D:], 0, win, bias, wout, slope, True
    )
    tan_out[...] = tan
    base, tan = base.astype(BF), tan.astype(BF)
    send_left[0] = base[0:B]
    send_left[1] = tan[0:B]
    send_right[0] = base[B:]
    send_right[1] = tan[B:]


def inner1_kernel(
    base_in, tan_in, lo0, lo1, hi0, hi1, field, a0, a1, a2, a3, nxt, win, bias, wout,
    amat, tmat, image, returned, hat, slope,
):
    y = member()
    sort_edges(y, (a0, a1, a2, a3), 1, amat, tmat)
    pair_matrix(amat, hat)
    for w in range(NW):
        lo, hi = (lo0, lo1)[w], (hi0, hi1)[w]
        base = stack(lo[0], base_in[w], hi[0])
        tan = stack(lo[1], tan_in[w].astype(BF), hi[1])
        base_sum = base_in[w].astype(F32) + dot(hat[...], base)
        tan_sum = tan_in[w] + dot(hat[...], tan)
        _, out = forward_rows(base_sum, tan_sum, 1, win, bias, wout, slope, False)
        image[w] = out.astype(BF)
        if w == 0:
            following = field[1, B : 3 * B, D:].astype(F32)
            current = following - out
        else:
            following = stack(nxt[1], nxt[2]).astype(F32)
            current = jnp.where(last_member(), 0.0, following - out)
        returned[w] = adjoint_rows(current, 1, win, wout, slope)


def edge1_kernel(
    lo0, lo1, hi0, hi1, tan0, tan1, left0, left1, right0, right1, base_in, tan_in, field, nxt, amat, tmat, image_in, win, bias, wout,
    image0, image1, returned, send_left, send_right, slope,
):
    for w in range(NW):
        lo, hi, tan_edge = (lo0, lo1)[w], (hi0, hi1)[w], (tan0, tan1)[w]
        left, right = (left0, left1)[w], (right0, right1)[w]
        tan_mid = tan_in[w].astype(BF)
        agg = []
        for f, mid in ((0, base_in[w]), (1, tan_mid)):
            agg.append(stack(
                dot(amat[0], stack(left[f], lo[f], mid[0:B])),
                dot(amat[G - 1], stack(mid[B:], hi[f], right[f])),
            ))
        base_sum = stack(lo[0], hi[0]).astype(F32) + agg[0]
        _, out = forward_rows(base_sum, tan_edge[...] + agg[1], 1, win, bias, wout, slope, False)
        image = (image0, image1)[w]
        image[0] = out[0:B].astype(BF)
        image[1] = image_in[w, 0:B]
        image[2] = image_in[w, B:]
        image[3] = out[B:].astype(BF)
        if w == 0:
            following = stack(field[1, 0:B, D:], field[1, 3 * B :, D:]).astype(F32)
            current = following - out
        else:
            current = jnp.where(last_member(), 0.0, stack(nxt[0], nxt[G - 1]).astype(F32) - out)
        back = adjoint_rows(current, 1, win, wout, slope)
        returned[w] = back
        send_left[w] = dot(tmat[0, :, 0:B], back[0:B].astype(BF)).astype(BF)
        send_right[w] = dot(tmat[G - 1, :, 2 * B :], back[B:].astype(BF)).astype(BF)


def spread_edge(tmat, edge, narrow):
    return edge + stack(
        dot(tmat[0, :, B:], narrow[0 : 2 * B]), dot(tmat[G - 1, :, 0 : 2 * B], narrow[2 * B :])
    )


def inner2_kernel(inner, edge, tmat, slope, win, wout, cur_edge, returned, hat):
    pair_matrix(tmat, hat)
    for w in range(NW):
        narrow = stack(edge[w, 0:B], inner[w], edge[w, B:]).astype(BF)
        cur_edge[w] = spread_edge(tmat, edge[w], narrow)
        current = inner[w] + dot(hat[...], narrow)
        returned[w] = adjoint_rows(current, 0, win, wout, slope.at[w])


def edge2_kernel(cur_edge, left, right, tmat, slope0, slope1, win, wout, returned, send_left, send_right):
    for w in range(NW):
        current = cur_edge[w] + stack(left[w], right[w]).astype(F32)
        back = adjoint_rows(current, 0, win, wout, (slope0, slope1)[w])
        returned[w] = back
        send_left[w] = dot(tmat[0, :, 0:B], back[0:B].astype(BF)).astype(BF)
        send_right[w] = dot(tmat[G - 1, :, 2 * B :], back[B:].astype(BF)).astype(BF)


def inner3_kernel(
    inner, edge, tmat, image0, image1, before, cur_edge, cur_inner, im0, im1, im2, im3, hat
):
    y = member()
    for k, im in enumerate((im0, im1, im2, im3)):
        block = lax.rem(y + k, G)
        im[0] = image0[block]
        im[1] = jnp.where(y == G - 1, before[block], image1[block])
    pair_matrix(tmat, hat)
    for w in range(NW):
        narrow = stack(edge[w, 0:B], inner[w], edge[w, B:]).astype(BF)
        cur_edge[w] = spread_edge(tmat, edge[w], narrow)
        cur_inner[w] = (inner[w] + dot(hat[...], narrow)).astype(BF)


def finish_kernel(cur_edge, cur_inner, left, right, o0, o1, o2, o3, all_blocks):
    y = member()
    for w in range(NW):
        all_blocks[0, w] = (cur_edge[w, 0:B] + left[w].astype(F32)).astype(BF)
        all_blocks[1, w] = cur_inner[w, 0:B]
        all_blocks[2, w] = cur_inner[w, B:]
        all_blocks[3, w] = (cur_edge[w, B:] + right[w].astype(F32)).astype(BF)
    for k, out in enumerate((o0, o1, o2, o3)):
        out[...] = all_blocks[lax.rem(y + k, G)]


def misfit_kernel(inc, i0, i1, i2, i3, misfit, kept):
    y = member()
    for k, im in enumerate((i0, i1, i2, i3)):
        m = origin(y, k)
        value = inc[NW * m + 1] - im[0].astype(F32)
        misfit[NW * m + 1] = value
        kept[NW * m + 1] = value
        even = NW * lax.rem(m + 1, G)
        value = inc[even] - im[1].astype(F32)
        misfit[even] = value
        kept[even] = value


def normal_kernel(kept, p0, p1, p2, p3, normal):
    y = member()
    for k, part in enumerate((p0, p1, p2, p3)):
        m = origin(y, k)
        for w in range(NW):
            normal[NW * m + w] = kept[NW * m + w] - part[w].astype(F32)


VMEM_LIMIT = 16 * 1024 * 1024
SMEM = pl.BlockSpec(memory_space=pltpu.SMEM)
VMEM = pl.BlockSpec(memory_space=pltpu.VMEM)


def sds(shape, dtype=BF):
    return jax.ShapeDtypeStruct(shape, dtype)


def call(kernel, ins, outs, scratch=(), smem=0):
    return pl.pallas_call(
        kernel,
        out_shape=outs,
        in_specs=[SMEM] * smem + [VMEM] * (len(ins) - smem),
        out_specs=[VMEM] * len(outs),
        scratch_shapes=list(scratch),
        compiler_params=pltpu.CompilerParams(vmem_limit_bytes=VMEM_LIMIT),
    )(*ins)


def group_pairs(k):
    return [(b, b // G * G + (b + k) % G) for b in range(PARTS)]


def side_pairs(d):
    return [(b, (b + G * d) % PARTS) for b in range(PARTS)]


def next_increment_pairs():
    pairs = []
    for t in range(TM):
        for b in range(PARTS):
            to = (t - 1) % TM if b % G == 0 else t
            pairs.append((t * PARTS + b, to * PARTS + b // G * G + (b - 1) % G))
    return pairs


def last_image_pairs():
    return [
        (t * PARTS + b, (t + 1) * PARTS + b)
        for t in range(TM - 1) for b in range(PARTS) if b % G == G - 1
    ]


def to_members(sends):
    return [lax.ppermute(sends[k], "mesh", group_pairs(k)) for k in range(1, G)]


def swap_sides(send_left, send_right):
    left = lax.ppermute(send_right, "mesh", side_pairs(1))
    right = lax.ppermute(send_left, "mesh", side_pairs(-1))
    return left, right


def local(states, increment, window_slots, edge_weights, inner_weight, inner_bias, outer_weight):

    item = sds((2, B, D))
    half = sds((NW, B, D))
    pair_bf = sds((NW, 2 * B, D))
    pair = sds((NW, 2 * B, D), F32)
    hidden = sds((NW, 2 * B, HID))
    mats = sds((G, B, 3 * B))
    hat = pltpu.VMEM((2 * B, 4 * B), BF)
    weights = (inner_weight, inner_bias, outer_weight)

    sends = call(pack_kernel, (states, increment), [item] * (NW * (G - 1)))
    got = [to_members([None, *sends[w * (G - 1) : (w + 1) * (G - 1)]]) for w in range(NW)]
    *own, folded = call(
        fold_kernel, (window_slots, states, increment, edge_weights),
        [item] * NW + [sds((B, 6 * B))], smem=1,
    )
    folded = [folded, *to_members([folded] * G)]

    got = [[own[w], *got[w]] for w in range(NW)]
    lo, hi, nxt = call(edge_kernel, got[0], [item, item, sds((G, B, D))])
    nxt = lax.ppermute(nxt, ("tm", "mesh"), next_increment_pairs())
    halo = [swap_sides(lo, hi)]
    lo, hi = call(edge_kernel, got[1], [item, item])
    halo.append(swap_sides(lo, hi))
    field, amat0, tmat0, base_in, tan_in, slope_in = call(
        inner0_kernel, (*got[0], *got[1], *folded, *weights),
        [sds((NW, G * B, 2 * D)), mats, mats, pair_bf, pair, hidden], (hat,),
    )
    lo, hi, tan_edge, slope_edge, left, right = [], [], [], [], [], []
    for w in range(NW):
        out = call(
            functools.partial(edge0_kernel, w), (field, amat0, *halo[w], *weights),
            [item, item, sds((2 * B, D), F32), sds((2 * B, HID))],
        )
        for values, value in zip((lo, hi, tan_edge, slope_edge), out):
            values.append(value)
        for values, value in zip((left, right), swap_sides(out[0], out[1])):
            values.append(value)

    slope1 = pltpu.VMEM((2 * B, HID), BF)
    amat1, tmat1, image_in, inner = call(
        inner1_kernel, (base_in, tan_in, *lo, *hi, field, *folded, nxt, *weights),
        [mats, mats, pair_bf, pair], (hat, slope1),
    )
    image0, image1, edge, send_left, send_right = call(
        edge1_kernel,
        (*lo, *hi, *tan_edge, *left, *right, base_in, tan_in, field, nxt, amat1, tmat1, image_in, *weights),
        [sds((G, B, D))] * NW + [pair, half, half], (slope1,),
    )

    left, right = swap_sides(send_left, send_right)
    before = lax.ppermute(image1, ("tm", "mesh"), last_image_pairs())
    cur_edge, inner = call(
        inner2_kernel, (inner, edge, tmat1, slope_in, inner_weight, outer_weight),
        [pair, pair], (hat,)
    )
    edge, send_left, send_right = call(
        edge2_kernel, (cur_edge, left, right, tmat0, *slope_edge, inner_weight, outer_weight),
        [pair, half, half]
    )

    left, right = swap_sides(send_left, send_right)
    cur_edge, cur_inner, *images = call(
        inner3_kernel, (inner, edge, tmat0, image0, image1, before),
        [pair, pair_bf] + [half] * G, (hat,),
    )
    images = [images[0], *to_members(images)]
    parts = call(
        finish_kernel, (cur_edge, cur_inner, left, right), [half] * G,
        (pltpu.VMEM((G, NW, B, D), BF),),
    )
    parts = [parts[0], *to_members(parts)]
    whole = sds(increment.shape, F32)
    misfit, kept = call(misfit_kernel, (increment, *images), [whole, whole])
    (normal,) = call(normal_kernel, (kept, *parts), [whole])
    return misfit, normal


def solution(mesh):
    placed = (
        P("tm", "mesh", None),
        P("tm", "mesh", None),
        P("mesh", None),
        P(None, "mesh", None, None, None),
        P(),
        P(),
        P(),
    )

    return jax.shard_map(
        local,
        mesh=mesh,
        in_specs=placed,
        out_specs=(P("tm", "mesh", None), P("tm", "mesh", None)),
        check_vma=False,
    )
```

```python
import functools

import jax
import jax.numpy as jnp
from jax import lax
from jax.experimental import pallas as pl
from jax.experimental.pallas import tpu as pltpu
from jax.sharding import PartitionSpec as P


BF = jnp.bfloat16
F32 = jnp.float32
G = 4
NW = 2
B = 128
D = 256
HID = 1024
HC = 256
TM = 4
PARTS = 64
HALF_ROOT = 0.7071067811865476
DENSITY_NORM = 0.3989422804014327


def dot(a, b, ca=1, cb=0):
    return lax.dot_general(a, b, (((ca,), (cb,)), ((), ())), preferred_element_type=F32)


def member():
    return lax.rem(lax.axis_index("mesh"), G)


def last_member():
    return jnp.logical_and(member() == G - 1, lax.axis_index("tm") == TM - 1)


def even_group():
    return lax.rem(lax.div(lax.axis_index("mesh"), G), 2) == 0


def swap(first, second):
    even = even_group()
    return jnp.where(even, first, second), jnp.where(even, second, first)


def origin(y, k):
    return lax.rem(y + G - k, G)


def stack(*values):
    return jnp.concatenate(values, axis=0)


def pack_kernel(states, inc, *outs):
    y = member()
    for w in range(NW):
        for k in range(1, G):
            m = lax.rem(y + k, G)
            outs[w * (G - 1) + k - 1][0] = states[NW * m + w]
            outs[w * (G - 1) + k - 1][1] = inc[NW * m + w].astype(BF)


def fold_kernel(slots, states, inc, edges, own0, own1, folded):
    y = member()
    for w, own in enumerate((own0, own1)):
        own[0] = states[NW * y + w]
        own[1] = inc[NW * y + w].astype(BF)
    for layer in range(2):
        for slot in range(3):
            total = jnp.zeros((B, B), F32)
            for f in range(4):
                total += jnp.where(slots[0, f] == slot, edges[layer, 0, f].astype(F32), 0.0)
            first = (3 * layer + slot) * B
            folded[:, first : first + B] = total.astype(BF)


def edge_kernel(r0, r1, r2, r3, far, near, inc=None):
    y = member()
    far_block = jnp.where(even_group(), 0, G - 1)
    for k, r in enumerate((r0, r1, r2, r3)):
        block = origin(y, k)
        if inc is not None:
            inc[block] = r[1]

        @pl.when(block == far_block)
        def _():
            far[...] = r[...]

        @pl.when(block == G - 1 - far_block)
        def _():
            near[...] = r[...]


def sort_edges(y, mats, layer, amat, tmat):
    for k, a in enumerate(mats):
        amat[origin(y, k)] = a[:, 3 * layer * B : 3 * (layer + 1) * B]
    for c in range(G):
        for slot in range(3):
            t = jnp.transpose(amat[c, :, slot * B : (slot + 1) * B].astype(F32)).astype(BF)
            to = c + slot - 1
            if 0 <= to < G:
                place = 2 - slot
            else:
                to, place = c, slot
            tmat[to, :, place * B : (place + 1) * B] = t


def pair_matrix(mats, hat):
    hat[0:B, 3 * B :] = jnp.zeros((B, B), BF)
    hat[B:, 0:B] = jnp.zeros((B, B), BF)
    hat[0:B, 0 : 3 * B] = mats[1]
    hat[B:, B:] = mats[2]


def forward_rows(base_sum, tan_sum, layer, win, bias, wout, slope, with_base):
    both = stack(base_sum.astype(BF), tan_sum.astype(BF))
    half = base_sum.shape[0]
    for h in range(HID // HC):
        cols = slice(h * HC, (h + 1) * HC)
        z = dot(both, win[layer, :, cols])
        act = z[:half] + bias[layer : layer + 1, cols]
        phi = 0.5 * (1.0 + lax.erf(act * HALF_ROOT))
        slp = phi + act * jnp.exp(-0.5 * act * act) * DENSITY_NORM
        slope[:, cols] = slp.astype(BF)
        lifted = (slp * z[half:]).astype(BF)
        tan_sum = tan_sum + dot(lifted, wout[layer, cols, :])
        if with_base:
            base_sum = base_sum + dot((act * phi).astype(BF), wout[layer, cols, :])
    return base_sum, tan_sum


def adjoint_rows(current, layer, win, wout, slope):
    narrow = current.astype(BF)
    for h in range(HID // HC):
        cols = slice(h * HC, (h + 1) * HC)
        up = dot(narrow, wout[layer, cols, :], 1, 1)
        pulled = (slope[:, cols].astype(F32) * up).astype(BF)
        current = current + dot(pulled, win[layer, :, cols], 1, 1)
    return current


def inner0_kernel(
    r00, r01, r02, r03, r10, r11, r12, r13, a0, a1, a2, a3, win, bias, wout,
    field, amat, tmat, base_out, tan_out, slope, hat,
):
    y = member()
    sort_edges(y, (a0, a1, a2, a3), 0, amat, tmat)
    pair_matrix(amat, hat)
    for w, got in enumerate(((r00, r01, r02, r03), (r10, r11, r12, r13))):
        for k, r in enumerate(got):
            rows = pl.ds(pl.multiple_of(origin(y, k) * B, B), B)
            field[w, rows, 0:D] = r[0]
            field[w, rows, D:] = r[1]
    for w in range(NW):
        agg = dot(hat[...], field[w])
        base_sum = field[w, B : 3 * B, 0:D].astype(F32) + agg[:, 0:D]
        tan_sum = field[w, B : 3 * B, D:].astype(F32) + agg[:, D:]
        base, tan = forward_rows(base_sum, tan_sum, 0, win, bias, wout, slope.at[w], True)
        base_out[w] = base.astype(BF)
        tan_out[w] = tan


def edge0_kernel(
    w, field, amat, far, near, win, bias, wout,
    send_far, send_near, tan_out, slope,
):
    left, right = zip(*(swap(far[f], near[f]) for f in range(2)))
    lo = stack(jnp.concatenate([left[0], left[1]], axis=1), field[w, 0 : 2 * B])
    hi = stack(field[w, 2 * B :], jnp.concatenate([right[0], right[1]], axis=1))
    agg = stack(dot(amat[0], lo), dot(amat[G - 1], hi))
    own = stack(field[w, 0:B], field[w, 3 * B :]).astype(F32)
    base, tan = forward_rows(
        own[:, 0:D] + agg[:, 0:D], own[:, D:] + agg[:, D:], 0, win, bias, wout, slope, True
    )
    tan_out[...] = tan
    base, tan = base.astype(BF), tan.astype(BF)
    send_far[0], send_near[0] = swap(base[0:B], base[B:])
    send_far[1], send_near[1] = swap(tan[0:B], tan[B:])


def inner1_kernel(
    base_in, tan_in, far0, far1, near0, near1, field, a0, a1, a2, a3, nxt, win, bias, wout,
    amat, tmat, image, returned, hat, slope,
):
    y = member()
    sort_edges(y, (a0, a1, a2, a3), 1, amat, tmat)
    pair_matrix(amat, hat)
    for w in range(NW):
        far, near = (far0, far1)[w], (near0, near1)[w]
        lo, hi = zip(*(swap(far[f], near[f]) for f in range(2)))
        base = stack(lo[0], base_in[w], hi[0])
        tan = stack(lo[1], tan_in[w].astype(BF), hi[1])
        base_sum = base_in[w].astype(F32) + dot(hat[...], base)
        tan_sum = tan_in[w] + dot(hat[...], tan)
        _, out = forward_rows(base_sum, tan_sum, 1, win, bias, wout, slope, False)
        image[w] = out.astype(BF)
        if w == 0:
            following = field[1, B : 3 * B, D:].astype(F32)
            current = following - out
        else:
            following = stack(nxt[1], nxt[2]).astype(F32)
            current = jnp.where(last_member(), 0.0, following - out)
        returned[w] = adjoint_rows(current, 1, win, wout, slope)


def edge1_kernel(
    far0, far1, near0, near1, tan0, tan1, got_far0, got_far1, got_near0, got_near1, base_in, tan_in, field, nxt, amat, tmat, image_in, win, bias, wout,
    im0, im1, im2, im3, returned, send_far, send_near, slope, image,
):
    y = member()
    for w in range(NW):
        far, near, tan_edge = (far0, far1)[w], (near0, near1)[w], (tan0, tan1)[w]
        lo, hi = zip(*(swap(far[f], near[f]) for f in range(2)))
        far, near = (got_far0, got_far1)[w], (got_near0, got_near1)[w]
        left, right = zip(*(swap(far[f], near[f]) for f in range(2)))
        tan_mid = tan_in[w].astype(BF)
        agg = []
        for f, mid in ((0, base_in[w]), (1, tan_mid)):
            agg.append(stack(
                dot(amat[0], stack(left[f], lo[f], mid[0:B])),
                dot(amat[G - 1], stack(mid[B:], hi[f], right[f])),
            ))
        base_sum = stack(lo[0], hi[0]).astype(F32) + agg[0]
        _, out = forward_rows(base_sum, tan_edge[...] + agg[1], 1, win, bias, wout, slope, False)
        image[0, w] = out[0:B].astype(BF)
        image[1, w] = image_in[w, 0:B]
        image[2, w] = image_in[w, B:]
        image[3, w] = out[B:].astype(BF)
        if w == 0:
            following = stack(field[1, 0:B, D:], field[1, 3 * B :, D:]).astype(F32)
            current = following - out
        else:
            current = jnp.where(last_member(), 0.0, stack(nxt[0], nxt[G - 1]).astype(F32) - out)
        back = adjoint_rows(current, 1, win, wout, slope)
        returned[w] = back
        send_far[w], send_near[w] = swap(
            dot(tmat[0, :, 0:B], back[0:B].astype(BF)).astype(BF),
            dot(tmat[G - 1, :, 2 * B :], back[B:].astype(BF)).astype(BF),
        )
    for k, im in enumerate((im0, im1, im2, im3)):
        im[...] = image[lax.rem(y + k, G)]


def spread_edge(tmat, edge, narrow):
    return edge + stack(
        dot(tmat[0, :, B:], narrow[0 : 2 * B]), dot(tmat[G - 1, :, 0 : 2 * B], narrow[2 * B :])
    )


def inner2_kernel(inner, edge, tmat, slope, win, wout, cur_edge, returned, hat):
    pair_matrix(tmat, hat)
    for w in range(NW):
        narrow = stack(edge[w, 0:B], inner[w], edge[w, B:]).astype(BF)
        cur_edge[w] = spread_edge(tmat, edge[w], narrow)
        current = inner[w] + dot(hat[...], narrow)
        returned[w] = adjoint_rows(current, 0, win, wout, slope.at[w])


def edge2_kernel(cur_edge, far, near, tmat, slope0, slope1, win, wout, returned, send_far, send_near):
    for w in range(NW):
        current = cur_edge[w] + stack(*swap(far[w], near[w])).astype(F32)
        back = adjoint_rows(current, 0, win, wout, (slope0, slope1)[w])
        returned[w] = back
        send_far[w], send_near[w] = swap(
            dot(tmat[0, :, 0:B], back[0:B].astype(BF)).astype(BF),
            dot(tmat[G - 1, :, 2 * B :], back[B:].astype(BF)).astype(BF),
        )


def inner3_kernel(inner, edge, tmat, i0, i1, i2, i3, cur_edge, cur_inner, last, hat):
    y = member()
    for k, im in enumerate((i0, i1, i2, i3)):

        @pl.when(origin(y, k) == G - 1)
        def _():
            last[...] = im[NW - 1]

    pair_matrix(tmat, hat)
    for w in range(NW):
        narrow = stack(edge[w, 0:B], inner[w], edge[w, B:]).astype(BF)
        cur_edge[w] = spread_edge(tmat, edge[w], narrow)
        cur_inner[w] = (inner[w] + dot(hat[...], narrow)).astype(BF)


def finish_kernel(cur_edge, cur_inner, far, near, o0, o1, o2, o3, all_blocks):
    y = member()
    for w in range(NW):
        left, right = swap(far[w], near[w])
        all_blocks[0, w] = (cur_edge[w, 0:B] + left.astype(F32)).astype(BF)
        all_blocks[1, w] = cur_inner[w, 0:B]
        all_blocks[2, w] = cur_inner[w, B:]
        all_blocks[3, w] = (cur_edge[w, B:] + right.astype(F32)).astype(BF)
    for k, out in enumerate((o0, o1, o2, o3)):
        out[...] = all_blocks[lax.rem(y + k, G)]


def misfit_kernel(inc, i0, i1, i2, i3, before, misfit, kept):
    y = member()
    for k, im in enumerate((i0, i1, i2, i3)):
        m = origin(y, k)
        value = inc[NW * m + 1] - im[0].astype(F32)
        misfit[NW * m + 1] = value
        kept[NW * m + 1] = value
        even = NW * lax.rem(m + 1, G)
        image = jnp.where(m == G - 1, before[...], im[1])
        value = inc[even] - image.astype(F32)
        misfit[even] = value
        kept[even] = value


def normal_kernel(kept, p0, p1, p2, p3, normal):
    y = member()
    for k, part in enumerate((p0, p1, p2, p3)):
        m = origin(y, k)
        for w in range(NW):
            normal[NW * m + w] = kept[NW * m + w] - part[w].astype(F32)


VMEM_LIMIT = 16 * 1024 * 1024
SMEM = pl.BlockSpec(memory_space=pltpu.SMEM)
VMEM = pl.BlockSpec(memory_space=pltpu.VMEM)


def sds(shape, dtype=BF):
    return jax.ShapeDtypeStruct(shape, dtype)


def call(kernel, ins, outs, scratch=(), smem=0):
    return pl.pallas_call(
        kernel,
        out_shape=outs,
        in_specs=[SMEM] * smem + [VMEM] * (len(ins) - smem),
        out_specs=[VMEM] * len(outs),
        scratch_shapes=list(scratch),
        compiler_params=pltpu.CompilerParams(vmem_limit_bytes=VMEM_LIMIT),
    )(*ins)


def group_pairs(k):
    return [(b, b // G * G + (b + k) % G) for b in range(PARTS)]


def side_pairs(near):
    pairs = []
    for b in range(PARTS):
        step = G if (b // G % 2 == 0) == near else -G
        pairs.append((b, (b + step) % PARTS))
    return pairs


def next_increment_pairs():
    pairs = []
    for t in range(TM):
        for b in range(PARTS):
            to = (t - 1) % TM if b % G == 0 else t
            pairs.append((t * PARTS + b, to * PARTS + b // G * G + (b - 1) % G))
    return pairs


def to_members(sends):
    return [lax.ppermute(sends[k], "mesh", group_pairs(k)) for k in range(1, G)]


def swap_sides(far, near):
    far = lax.ppermute(far, "mesh", side_pairs(False))
    near = lax.ppermute(near, "mesh", side_pairs(True))
    return far, near


def local(states, increment, window_slots, edge_weights, inner_weight, inner_bias, outer_weight):

    item = sds((2, B, D))
    half = sds((NW, B, D))
    pair_bf = sds((NW, 2 * B, D))
    pair = sds((NW, 2 * B, D), F32)
    hidden = sds((NW, 2 * B, HID))
    mats = sds((G, B, 3 * B))
    hat = pltpu.VMEM((2 * B, 4 * B), BF)
    weights = (inner_weight, inner_bias, outer_weight)

    sends = call(pack_kernel, (states, increment), [item] * (NW * (G - 1)))
    got = [to_members([None, *sends[w * (G - 1) : (w + 1) * (G - 1)]]) for w in range(NW)]
    *own, folded = call(
        fold_kernel, (window_slots, states, increment, edge_weights),
        [item] * NW + [sds((B, 6 * B))], smem=1,
    )
    folded = [folded, *to_members([folded] * G)]

    got = [[own[w], *got[w]] for w in range(NW)]
    lo, hi, nxt = call(edge_kernel, got[0], [item, item, sds((G, B, D))])
    halo = [swap_sides(lo, hi)]
    lo, hi = call(edge_kernel, got[1], [item, item])
    halo.append(swap_sides(lo, hi))
    nxt = lax.ppermute(nxt, ("tm", "mesh"), next_increment_pairs())
    field, amat0, tmat0, base_in, tan_in, slope_in = call(
        inner0_kernel, (*got[0], *got[1], *folded, *weights),
        [sds((NW, G * B, 2 * D)), mats, mats, pair_bf, pair, hidden], (hat,),
    )
    lo, hi, tan_edge, slope_edge, left, right = [], [], [], [], [], []
    for w in range(NW):
        out = call(
            functools.partial(edge0_kernel, w), (field, amat0, *halo[w], *weights),
            [item, item, sds((2 * B, D), F32), sds((2 * B, HID))],
        )
        for values, value in zip((lo, hi, tan_edge, slope_edge), out):
            values.append(value)
        for values, value in zip((left, right), swap_sides(out[0], out[1])):
            values.append(value)

    slope1 = pltpu.VMEM((2 * B, HID), BF)
    amat1, tmat1, image_in, inner = call(
        inner1_kernel, (base_in, tan_in, *lo, *hi, field, *folded, nxt, *weights),
        [mats, mats, pair_bf, pair], (hat, slope1),
    )
    *images, edge, send_left, send_right = call(
        edge1_kernel,
        (*lo, *hi, *tan_edge, *left, *right, base_in, tan_in, field, nxt, amat1, tmat1, image_in, *weights),
        [half] * G + [pair, half, half], (slope1, pltpu.VMEM((G, NW, B, D), BF)),
    )

    left, right = swap_sides(send_left, send_right)
    images = [images[0], *to_members(images)]
    cur_edge, inner = call(
        inner2_kernel, (inner, edge, tmat1, slope_in, inner_weight, outer_weight),
        [pair, pair], (hat,)
    )
    edge, send_left, send_right = call(
        edge2_kernel, (cur_edge, left, right, tmat0, *slope_edge, inner_weight, outer_weight),
        [pair, half, half]
    )

    left, right = swap_sides(send_left, send_right)
    cur_edge, cur_inner, last = call(
        inner3_kernel, (inner, edge, tmat0, *images), [pair, pair_bf, sds((B, D))], (hat,),
    )
    before = lax.ppermute(last, "tm", [(t, t + 1) for t in range(TM - 1)])
    parts = call(
        finish_kernel, (cur_edge, cur_inner, left, right), [half] * G,
        (pltpu.VMEM((G, NW, B, D), BF),),
    )
    parts = [parts[0], *to_members(parts)]
    whole = sds(increment.shape, F32)
    misfit, kept = call(misfit_kernel, (increment, *images, before), [whole, whole])
    (normal,) = call(normal_kernel, (kept, *parts), [whole])
    return misfit, normal


def solution(mesh):
    placed = (
        P("tm", "mesh", None),
        P("tm", "mesh", None),
        P("mesh", None),
        P(None, "mesh", None, None, None),
        P(),
        P(),
        P(),
    )

    return jax.shard_map(
        local,
        mesh=mesh,
        in_specs=placed,
        out_specs=(P("tm", "mesh", None), P("tm", "mesh", None)),
        check_vma=False,
    )
```
